512 devices in a mesh: ctx: 64 (over z, y), head: 8 (over x, core).
Axes of the slice: x: 4, y: 8, z: 8, core: 2. Of those that a mesh axis runs over, the one named last changes fastest.
Arguments:
- token_inputs: bfloat16 [32768, 8192], P(('ctx', 'head')), may hold values from -6 to 6
- state_in: bfloat16 [32768, 128], P(('ctx', 'head')), may hold values from -0.059814453 to 0.059814453
- state_out: bfloat16 [32768, 128], P(('ctx', 'head')), may hold values from -0.5 to 0.5
- log_decay: bfloat16 [32768, 128], P(('ctx', 'head')), may hold values from -1 to 0
- token_codes: int32 [32768], P(('ctx', 'head')), may hold values from 0 to 63
- level_table: bfloat16 [64, 1408], replicated, may hold values from 0.099609375 to 1
- skip_gain: float32 [128], replicated, may hold values from 0.2 to 1
Outputs:
- mixed_output: bfloat16 [32768, 8192], P(('ctx', 'head'))
The draws below stay inside these ranges and needn't reach their ends.
All inputs are finite; a program needn't handle non-finite values.
Results may differ from the reference program's by a relative error of at most 0.009.
Values may be sent and summed in bfloat16 or wider, within the bound.
A program may use at most 64 MiB of HBM per device.

```python
import math
import jax
import jax.numpy as jnp
import numpy as np
from jax import lax

COUNT_OF_HEADS = 128
HEAD_DIM = 64
STATE = 128
SPAN = 64
LEVELS = 11
CODES = 64
TOK_DEV = 64
BLOCK_TOKENS = 512
SEQUENCE_BLOCKS = 64
WINDOW_TOKENS = 32768
N_CTX = 64


def draw_log_decay(key, part):
    key_matrix_rows = jax.random.split(key, 9)
    rapid_count = COUNT_OF_HEADS // 5
    moderate_count = COUNT_OF_HEADS // 5
    spike_count = COUNT_OF_HEADS // 5
    head_ordering = jax.random.permutation(key_matrix_rows[0], COUNT_OF_HEADS)
    is_quick_decay = head_ordering < rapid_count
    is_medium = (head_ordering >= rapid_count) & (head_ordering < rapid_count + moderate_count)
    is_spiky = (head_ordering >= rapid_count + moderate_count) & (head_ordering < rapid_count + moderate_count + spike_count)
    fast_rate = jax.random.uniform(key_matrix_rows[1], (COUNT_OF_HEADS,), minval=1.0 / 50.0, maxval=1.0 / 30.0)
    medium_rate = jax.random.uniform(key_matrix_rows[7], (COUNT_OF_HEADS,), minval=0.6, maxval=1.0) / BLOCK_TOKENS
    slow_rate = jnp.exp(jax.random.uniform(key_matrix_rows[2], (COUNT_OF_HEADS,), minval=math.log(0.3), maxval=math.log(1.2))) / WINDOW_TOKENS
    rate = jnp.where(is_quick_decay, fast_rate, jnp.where(is_medium, medium_rate, slow_rate))
    blocks = WINDOW_TOKENS // TOK_DEV
    device_factor = jnp.exp(jax.random.uniform(key_matrix_rows[3], (blocks, 1, COUNT_OF_HEADS), minval=math.log(0.5), maxval=math.log(2.0)))
    roughness = jax.random.uniform(key_matrix_rows[4], (blocks, TOK_DEV, COUNT_OF_HEADS), minval=0.5, maxval=1.5)
    total_amount = (rate[None, None, :] * device_factor * roughness).reshape(WINDOW_TOKENS, COUNT_OF_HEADS)
    spike_rows = jax.random.randint(key_matrix_rows[5], (2, COUNT_OF_HEADS), 0, WINDOW_TOKENS)
    retain_factor = jax.random.uniform(key_matrix_rows[6], (2, COUNT_OF_HEADS), minval=0.6, maxval=0.8)
    token_positions = jnp.arange(WINDOW_TOKENS)[:, None]
    spike_groups = jnp.zeros((WINDOW_TOKENS, COUNT_OF_HEADS), jnp.float32)
    for spike_index in range(2):
        spike_groups = spike_groups + jnp.where(token_positions == spike_rows[spike_index][None, :], -jnp.log(retain_factor[spike_index])[None, :], 0.0)
    spike_groups = jnp.where(is_quick_decay[None, :], 0.0, spike_groups)
    value_rows = -(total_amount + spike_groups)
    block_number_index = token_positions // BLOCK_TOKENS
    within_block_index = token_positions % BLOCK_TOKENS
    spike_offset = jax.random.randint(key_matrix_rows[8], (COUNT_OF_HEADS,), 0, min(8, SEQUENCE_BLOCKS))
    spike_row_set = (block_number_index % 8 == spike_offset[None, :]) & (within_block_index >= BLOCK_TOKENS - 3) & is_spiky[None, :]
    value_rows = jnp.where(spike_row_set, -1.0, value_rows)
    return value_rows.astype(jnp.bfloat16)


def plant(result, rng, low, top_value):
    longest = result.shape.index(max(result.shape))
    spots = []
    for shift in (0, 1):
        where = [jax.random.randint(jax.random.fold_in(rng, axis), (), 0, length) for axis, length in enumerate(result.shape)]
        where[longest] = (where[longest] + shift) % result.shape[longest]
        spots.append(tuple(where))
    return result.at[spots[0]].set(low).at[spots[1]].set(top_value)


def block_levels(stream_key, dims, pieces, least, top_value):
    gain = 1.0
    for dim, parts in pieces:
        steps = jax.random.uniform(jax.random.fold_in(jax.random.fold_in(stream_key, 6), dim), (parts,), jnp.float32, least / len(pieces), top_value / len(pieces))
        gain = gain * jnp.repeat(jnp.exp(steps), dims[dim] // parts).reshape((-1,) + (1,) * (len(dims) - 1 - dim))
    return gain


def cumulative_ranks(number_of, skew):
    loads = [(1 << 20) // math.isqrt(standing ** skew) + 1 for standing in range(1, number_of + 1)]
    spread = 1 + sum(loads) // (1 << 30)
    return np.cumsum(np.array([max(1, weight // spread) for weight in loads]))


def ranked_ids(key, shape, number_of, skew):
    table = cumulative_ranks(number_of, skew)
    pick = jax.random.randint(jax.random.fold_in(key, 1), shape, 0, int(table[number_of - 1]))
    grade = jnp.searchsorted(jnp.asarray(table, jnp.int32), pick, side="right")
    return jax.random.permutation(jax.random.fold_in(key, 2), number_of)[grade].astype(jnp.int32)


def bell_draw(rng, dims, width, limit, pieces=(), kind=jnp.bfloat16):
    factor_of = block_levels(rng, dims, pieces, -0.22, 0.18) if pieces else 1.0
    drawn = jax.random.normal(rng, dims, jnp.float32) * width * factor_of
    return jnp.minimum(jnp.maximum(drawn, -limit), limit).astype(kind)


def setup_inputs(seed: int = 0) -> dict:
    streams_of = jax.random.split(jax.random.key(seed), 8)
    token_inputs = bell_draw(streams_of[0], (WINDOW_TOKENS, COUNT_OF_HEADS * HEAD_DIM), 1.0, 6.0, ((0, 512),))
    state_in = bell_draw(streams_of[1], (WINDOW_TOKENS, STATE), 0.01, 0.059814453, ((0, 512),))
    state_out = bell_draw(streams_of[2], (WINDOW_TOKENS, STATE), STATE ** -0.5, 0.5, ((0, 512),))
    log_decay = draw_log_decay(jax.random.fold_in(streams_of[7], 71), 0)
    token_codes = plant(ranked_ids(streams_of[4], (WINDOW_TOKENS,), CODES, 2), jax.random.fold_in(streams_of[4], 3), 0, CODES - 1).astype(jnp.int32)
    level_table = jnp.clip(jnp.exp(jax.random.uniform(streams_of[5], (CODES, COUNT_OF_HEADS * LEVELS), jnp.float32, math.log(0.099609375), math.log(1.0))), 0.099609375, 1.0).astype(jnp.bfloat16)
    skip_gain = jnp.clip(jnp.exp(jax.random.uniform(streams_of[6], (COUNT_OF_HEADS,), jnp.float32, math.log(0.2), math.log(1.0))), 0.2, 1.0)
    return dict(token_inputs=token_inputs, state_in=state_in, state_out=state_out, log_decay=log_decay, token_codes=token_codes, level_table=level_table, skip_gain=skip_gain)


def look_up(token_codes, weight_table):
    one_hot = (token_codes[:, None] == jnp.arange(weight_table.shape[0], dtype=jnp.int32)[None, :]).astype(jnp.bfloat16)
    return jnp.dot(one_hot, weight_table, preferred_element_type=jnp.float32).astype(jnp.bfloat16)


def level_onehot(spans, levels):
    span_ids = jnp.arange(spans, dtype=jnp.int32)
    xored = jnp.bitwise_xor(span_ids[:, None], span_ids[None, :])
    level_ids = jnp.zeros((spans, spans), jnp.int32)
    for level_bit in range(max(spans.bit_length() - 1, 0)):
        level_ids = level_ids + (xored >= (1 << level_bit)).astype(jnp.int32)
    return (level_ids[:, :, None] == jnp.arange(levels, dtype=jnp.int32)[None, None, :]).astype(jnp.float32)


def head_local(scores, head_input, head_weights, head_running, onehot, span):
    block_rows = head_input.shape[0]
    spans = block_rows // span
    weight_blocks = head_weights.astype(jnp.float32).reshape(spans, span, -1)
    pair_weights = jnp.einsum("iql,ijl->iqj", weight_blocks, onehot, precision=lax.Precision.HIGHEST)
    row_weights = jnp.broadcast_to(pair_weights.reshape(block_rows, spans, 1), (block_rows, spans, span)).reshape(block_rows, block_rows)
    position = jnp.arange(block_rows)
    causal = position[:, None] >= position[None, :]
    log_gap = jnp.where(causal, head_running[:, None] - head_running[None, :], 0.0)
    decay_factor = jnp.where(causal, jnp.exp(log_gap), 0.0)
    weight = (row_weights * decay_factor * scores).astype(jnp.bfloat16)
    return jnp.dot(weight, head_input, preferred_element_type=jnp.float32)


def head_state(head_input, head_running, state_in):
    carried = jnp.exp(head_running[-1] - head_running)[:, None] * head_input.astype(jnp.float32)
    return jnp.einsum("tn,tp->np", state_in, carried.astype(jnp.bfloat16), preferred_element_type=jnp.float32)


def finish(local_part, head_input, head_weights, head_running, state_out, bucket_states, skip_value, span_bits, ctx_bits):
    reached = jnp.einsum("tn,mnp->tmp", state_out, bucket_states, preferred_element_type=jnp.float32)
    factors = head_weights[:, span_bits + 1:span_bits + 1 + ctx_bits].astype(jnp.float32) * jnp.exp(head_running)[:, None]
    cross_part = jnp.sum(factors[:, :, None] * reached, axis=1)
    return (local_part + cross_part + skip_value * head_input.astype(jnp.float32)).astype(jnp.bfloat16)


def reference(token_inputs, state_in, state_out, log_decay, token_codes, level_table, skip_gain):
    heads = skip_gain.shape[0]
    head_dim = token_inputs.shape[1] // heads
    levels = level_table.shape[1] // heads
    block_rows = WINDOW_TOKENS // N_CTX
    spans = block_rows // SPAN
    span_bits = spans.bit_length() - 1
    ctx_bits = N_CTX.bit_length() - 1
    onehot = level_onehot(spans, levels)
    weights_all = look_up(token_codes, level_table).reshape(N_CTX, block_rows, heads, levels)
    input_blocks = token_inputs.reshape(N_CTX, block_rows, heads, head_dim)
    in_blocks = state_in.reshape(N_CTX, block_rows, -1)
    out_blocks = state_out.reshape(N_CTX, block_rows, -1)
    running_all = jnp.cumsum(log_decay.reshape(N_CTX, block_rows, heads).astype(jnp.float32), axis=1)

    def summarize(inputs):
        input_block, in_block, running = inputs

        def per_head(head_index):
            return head_state(input_block[:, head_index], running[:, head_index], in_block)
        return lax.map(per_head, jnp.arange(heads))

    states = lax.map(summarize, (input_blocks, in_blocks, running_all))
    summary = states
    summary_decay = running_all[:, -1]
    device = jnp.arange(N_CTX, dtype=jnp.int32)
    inside = jnp.zeros((N_CTX, heads), jnp.float32)
    buckets = []
    for level_bit in range(ctx_bits):
        sibling = jnp.bitwise_xor(device >> level_bit, 1)
        is_upper = ((device >> level_bit) & 1) == 1
        partner = summary[sibling]
        partner_decay = summary_decay[sibling]
        buckets.append(jnp.where(is_upper[:, None, None, None], partner * jnp.exp(inside)[:, :, None, None], 0.0).astype(jnp.bfloat16))
        inside = jnp.where(is_upper[:, None], inside + partner_decay, inside)
        summary = summary[0::2] * jnp.exp(summary_decay[1::2])[:, :, None, None] + summary[1::2]
        summary_decay = summary_decay[0::2] + summary_decay[1::2]
    bucket_all = jnp.stack(buckets, axis=1)

    def produce(inputs):
        input_block, in_block, out_block, running, weights, bucket_block = inputs
        scores = jnp.einsum("tn,sn->ts", out_block, in_block, preferred_element_type=jnp.float32)

        def per_head(head_index):
            local_part = head_local(scores, input_block[:, head_index], weights[:, head_index], running[:, head_index], onehot, SPAN)
            return finish(local_part, input_block[:, head_index], weights[:, head_index], running[:, head_index], out_block, bucket_block[:, head_index], skip_gain[head_index], span_bits, ctx_bits)
        mixed_rows = lax.map(per_head, jnp.arange(heads))
        return jnp.moveaxis(mixed_rows, 0, 1).reshape(block_rows, heads * head_dim)

    mixed_blocks = lax.map(produce, (input_blocks, in_blocks, out_blocks, running_all, weights_all, bucket_all))
    return mixed_blocks.reshape(WINDOW_TOKENS, heads * head_dim)
```

```python
import functools

import jax
import jax.numpy as jnp
from jax import lax
from jax.experimental import pallas as pl
from jax.experimental.pallas import tpu as pltpu
from jax.sharding import PartitionSpec as P

HEADS = 128
HEAD_DIM = 64
STATE = 128
SPAN = 64
LEVELS = 11
CODES = 64
NY = 8
LANES = 128
MESH = pl.DeviceIdType.MESH
F32 = jnp.float32
BF16 = jnp.bfloat16


def bits_of(n):
    return n.bit_length() - 1


def dot(a, b):
    return jnp.dot(a, b, preferred_element_type=F32)


def dot_t(a, b):
    return lax.dot_general(a, b, (((0,), (0,)), ((), ())), preferred_element_type=F32)


def iota(shape, dim):
    return lax.broadcasted_iota(jnp.int32, shape, dim)


def spread(v, first):
    idx = first + (iota(v.shape, 1) >> 6)
    return jnp.take_along_axis(v, idx, axis=1, mode="promise_in_bounds")


def kernel(
    nh, ny, nz,
    x, b, c, d, codes, tab, skip, out,
    xc, xr, br, cr, aux, auxr, o0, rows, te, oh, we, sg, lbs, li,
    sb, r1, pb, tz, r2, yb, zb, bks, tau, lt, pg, io, ir,
    xs, bs, cs, axs, taus, lts, r1s, l0s, ys, r2s, ags, ios,
):
    hl = HEADS // nh
    groups = hl // 2
    gp = groups // ny
    hbits, ybits, zbits = bits_of(nh), bits_of(ny), bits_of(nz)
    nlev = hbits + ybits + zbits
    hd = lax.axis_index("head")
    k = lax.axis_index("ctx")
    y = lax.rem(k, ny)
    z = lax.div(k, ny)

    def to_head(j):
        return {"head": j}

    def to_y(j):
        return {"ctx": z * ny + j}

    def to_z(j):
        return {"ctx": j * ny + y}

    def remote(src, dst, send, recv, where):
        return pltpu.make_async_remote_copy(
            src_ref=src, dst_ref=dst, send_sem=send, recv_sem=recv,
            device_id=where, device_id_type=MESH,
        )

    heads_round = [lax.rem(hd + i, nh) for i in range(1, nh)]
    y_round = [lax.rem(y + i, ny) for i in range(1, ny)]
    z_round = [lax.rem(z + i, nz) for i in range(1, nz)]

    lt[...] = jnp.zeros_like(lt)
    barrier = pltpu.get_barrier_semaphore()
    for j in heads_round:
        pl.semaphore_signal(barrier, inc=1, device_id=to_head(j), device_id_type=MESH)
    for j in y_round:
        pl.semaphore_signal(barrier, inc=1, device_id=to_y(j), device_id_type=MESH)
    for j in z_round:
        pl.semaphore_signal(barrier, inc=1, device_id=to_z(j), device_id_type=MESH)

    lower = iota((SPAN, SPAN), 0) >= iota((SPAN, SPAN), 1)
    run = dot(jnp.where(lower, 1.0, 0.0).astype(BF16), d[...])
    tot = run[SPAN - 1:SPAN, :]
    fac = jnp.exp(tot - run)

    pairs = HEADS // 2
    first = 2 * iota((pairs, LANES), 0) + (iota((pairs, LANES), 1) >> 6)
    tot_pairs = jnp.take_along_axis(
        jnp.broadcast_to(tot, (pairs, LANES)), first, axis=1, mode="promise_in_bounds"
    )
    code_row = codes[...].astype(F32)
    for j in range(nh):
        aux[j, 0:groups, :] = tot_pairs[j * groups:(j + 1) * groups, :]
        aux[j, groups:groups + 8, 0:SPAN] = jnp.broadcast_to(code_row, (8, SPAN))
        aux[j, groups:groups + 8, SPAN:] = jnp.zeros((8, LANES - SPAN), F32)
    auxr[hd] = aux[hd]
    br[hd] = b[...]
    cr[hd] = c[...]

    def carry(j):
        def one(p, _):
            cols = pl.ds(pl.multiple_of(p * LANES, LANES), LANES)
            src = pl.ds(pl.multiple_of((j * groups + p) * LANES, LANES), LANES)
            m = spread(fac, 2 * (j * groups + p))
            xc[j, :, cols] = (m * x[:, src].astype(F32)).astype(BF16)
            return 0

        lax.fori_loop(0, groups, one, 0, unroll=4)

    def send_x(j):
        return remote(xc.at[j], xr.at[hd], xs.at[0, j], xs.at[1, hd], to_head(j))

    def send_b(j):
        return remote(b, br.at[hd], bs.at[0, j], bs.at[1, hd], to_head(j))

    def send_c(j):
        return remote(c, cr.at[hd], cs.at[0, j], cs.at[1, hd], to_head(j))

    def send_a(j):
        return remote(aux.at[j], auxr.at[hd], axs.at[0, j], axs.at[1, hd], to_head(j))

    def send_o(j):
        return remote(io.at[j], ir.at[hd], ios.at[0, j], ios.at[1, hd], to_head(j))

    carry(heads_round[0])
    pl.semaphore_wait(barrier, (nh - 1) + (ny - 1) + (nz - 1))
    for j in heads_round:
        send_a(j).start()
    for j in heads_round:
        send_b(j).start()
    for i, j in enumerate(heads_round):
        if i:
            carry(j)
        send_x(j).start()
    for j in heads_round:
        send_c(j).start()
    carry(hd)
    xr[hd] = xc[hd]

    def recv_a(j):
        return remote(aux.at[j], auxr.at[j], axs.at[0, j], axs.at[1, j], to_head(j))

    for j in heads_round:
        recv_a(j).wait_recv()
    mine = auxr[0, 0:groups, :]
    for g in range(nh):
        pg[g] = jnp.exp(mine) if g else jnp.ones((groups, LANES), F32)
        if g:
            mine = mine + auxr[g, 0:groups, :]
    tau[y] = mine

    def send_tau(j):
        return remote(tau.at[y], tau.at[y], taus.at[0, j], taus.at[1, y], to_y(j))

    def recv_tau(j):
        return remote(tau.at[j], tau.at[j], taus.at[0, j], taus.at[1, j], to_y(j))

    for j in y_round:
        send_tau(j).start()

    cols0 = iota((LEVELS * HEADS, LANES), 0)
    lane0 = iota((LEVELS * HEADS, LANES), 1)
    tab0 = dot(tab[...], jnp.where(cols0 == lane0 * LEVELS, 1.0, 0.0).astype(BF16)).astype(BF16)
    code_t = jnp.where(
        jnp.broadcast_to(code_row, (CODES, SPAN)) == iota((CODES, SPAN), 0).astype(F32), 1.0, 0.0
    ).astype(BF16)
    w0 = dot_t(code_t, tab0)
    rows[0] = w0 * jnp.exp(run - tot)
    rows[1] = jnp.exp(run)

    per = LANES // hl
    for t in range(-(-nlev // per)):
        lev = 1 + t * per + lane0 // hl
        want = (hd * hl + lax.rem(lane0, hl)) * LEVELS + lev
        picked = dot(tab[...], jnp.where(cols0 == want, 1.0, 0.0).astype(BF16))
        for l in range(t * per, min(nlev, (t + 1) * per)):
            for p in range(groups):
                te[l, :, p * LANES:(p + 1) * LANES] = spread(
                    picked, (l - t * per) * hl + 2 * p
                ).astype(BF16)
    eye = jnp.where(iota((CODES, CODES), 0) == iota((CODES, CODES), 1), 1.0, 0.0).astype(BF16)
    for g in range(nh):
        row = auxr[g, groups:groups + 1, 0:SPAN]
        hot = jnp.where(
            jnp.broadcast_to(row, (CODES, SPAN)) == iota((CODES, SPAN), 0).astype(F32), 1.0, 0.0
        ).astype(BF16)
        oh[g * SPAN:(g + 1) * SPAN, :] = dot_t(hot, eye).astype(BF16)

    scores = lax.dot_general(
        c[...], b[...], (((1,), (1,)), ((), ())), preferred_element_type=F32
    )
    near = jnp.where(lower, scores, 0.0).astype(BF16)
    gain = jnp.broadcast_to(skip[...], (SPAN, LANES))

    def level0(j, _):
        v = dot(near, xc[j])
        for p in range(groups):
            cols = pl.ds(pl.multiple_of((j * groups + p) * LANES, LANES), LANES)
            at = 2 * (j * groups + p)
            o0[:, cols] = (
                spread(rows[0], at) * v[:, p * LANES:(p + 1) * LANES]
                + spread(gain, at) * x[:, cols].astype(F32)
            )
        return 0

    lax.fori_loop(0, nh, level0, 0)

    for j in y_round:
        recv_tau(j).wait_recv()
    line = tau[0]
    for j in range(1, ny):
        line = line + tau[j]
    lt[z] = line

    def send_lt(i):
        return remote(lt.at[z], lt.at[z], lts.at[0, z + i], lts.at[1, z], to_z(z + i))

    def recv_lt(i):
        return remote(lt.at[z], lt.at[z - i], lts.at[0, z], lts.at[1, z - i], to_z(z - i))

    for i in range(1, nz):
        @pl.when(z + i < nz)
        def _():
            send_lt(i).start()

    def recv_x(j):
        return remote(xc.at[j], xr.at[j], xs.at[0, j], xs.at[1, j], to_head(j))

    def recv_b(j):
        return remote(b, br.at[j], bs.at[0, j], bs.at[1, j], to_head(j))

    sg[hd] = dot_t(br[hd], xr[hd])
    for j in heads_round:
        recv_b(j).wait_recv()
    for j in heads_round:
        recv_x(j).wait_recv()
        sg[j] = dot_t(br[j], xr[j])

    offs = [0]
    for m in range(hbits):
        offs.append(offs[-1] + (nh >> (m + 1)))

    def fold(p, _):
        cols = pl.ds(pl.multiple_of(p * LANES, LANES), LANES)
        cur = [sg[g, :, cols] for g in range(nh)]
        dec = [auxr[g, pl.ds(p, 1), :] for g in range(nh)]
        for m in range(hbits):
            new, new_dec = [], []
            for i in range(len(cur) // 2):
                lbs[offs[m] + i, :, cols] = cur[2 * i].astype(BF16)
                new.append(cur[2 * i] * jnp.exp(dec[2 * i + 1]) + cur[2 * i + 1])
                new_dec.append(dec[2 * i] + dec[2 * i + 1])
            cur, dec = new, new_dec
        sb[p] = cur[0].astype(BF16)
        return 0

    lax.fori_loop(0, groups, fold, 0)

    def send_r1(j):
        return remote(
            sb.at[pl.ds(j * gp, gp)], r1.at[y], r1s.at[0, j], r1s.at[1, y], to_y(j)
        )

    def recv_r1(j):
        return remote(sb.at[pl.ds(j * gp, gp)], r1.at[j], r1s.at[0, j], r1s.at[1, j], to_y(j))

    for j in y_round:
        send_r1(j).start()

    def send_l0():
        return remote(sb, yb.at[0], l0s.at[0], l0s.at[1], to_y(y + 1))

    def recv_l0():
        return remote(sb, yb.at[0], l0s.at[0], l0s.at[1], to_y(y - 1))

    @pl.when(lax.rem(y, 2) == 0)
    def _():
        send_l0().start()

    for q in range(gp):
        r1[y, q] = sb[y * gp + q]

    for l in range(nlev):
        for g in range(0, nh, 2):
            w = dot(oh[g * SPAN:(g + 2) * SPAN, :], te[l]).astype(BF16)
            we[l, g] = w[0:SPAN]
            we[l, g + 1] = w[SPAN:]

    for i in range(1, nz):
        @pl.when(z - i >= 0)
        def _():
            recv_lt(i).wait_recv()
    for j in y_round:
        recv_r1(j).wait_recv()

    yoffs = [0]
    for m in range(1, ybits):
        yoffs.append(yoffs[-1] + (ny >> (m + 1)))
    for q in range(gp):
        cur = [r1[j, q].astype(F32) for j in range(ny)]
        dec = [tau[j, pl.ds(y * gp + q, 1), :] for j in range(ny)]
        for m in range(ybits):
            new, new_dec = [], []
            for i in range(len(cur) // 2):
                if m:
                    pb[yoffs[m - 1] + i, q] = cur[2 * i].astype(BF16)
                new.append(cur[2 * i] * jnp.exp(dec[2 * i + 1]) + cur[2 * i + 1])
                new_dec.append(dec[2 * i] + dec[2 * i + 1])
            cur, dec = new, new_dec
        r2[z, q] = cur[0].astype(BF16)
        tz[q] = cur[0].astype(BF16)

    def send_r2(i):
        return remote(tz, r2.at[z], r2s.at[0, z + i], r2s.at[1, z], to_z(z + i))

    def recv_r2(i):
        return remote(tz, r2.at[z - i], r2s.at[0, z], r2s.at[1, z - i], to_z(z - i))

    for i in range(1, nz):
        @pl.when(z + i < nz)
        def _():
            send_r2(i).start()

    def bit(v, m):
        return lax.rem(lax.div(v, 1 << m), 2) == 1

    def send_yb(m, j):
        return remote(
            pb.at[yoffs[m - 1] + lax.div(j, 2 << m)], yb.at[m, pl.ds(y * gp, gp)],
            ys.at[0, m, j], ys.at[1, m, y], to_y(j),
        )

    def recv_yb(m, j):
        return remote(
            pb.at[0], yb.at[m, pl.ds(j * gp, gp)], ys.at[0, m, j], ys.at[1, m, j], to_y(j)
        )

    for m in range(1, ybits):
        for j in y_round:
            @pl.when(bit(j, m))
            def _():
                send_yb(m, j).start()

        @pl.when(bit(y, m))
        def _():
            for q in range(gp):
                yb[m, y * gp + q] = pb[yoffs[m - 1] + lax.div(y, 2 << m), q]

    def recv_c(j):
        return remote(c, cr.at[j], cs.at[0, j], cs.at[1, j], to_head(j))

    for j in heads_round:
        recv_c(j).wait_recv()
    for g in range(nh):
        acc = [None] * groups
        for m in range(hbits):
            if not g >> m & 1:
                continue
            v = dot(cr[g], lbs[offs[m] + (g >> (m + 1))])
            gap = None
            for before in range(g >> m << m, g):
                row = auxr[before, 0:groups, :]
                gap = row if gap is None else gap + row
            scale = None if gap is None else jnp.exp(gap)
            for p in range(groups):
                cols = slice(p * LANES, (p + 1) * LANES)
                term = we[m, g, :, cols].astype(F32) * v[:, cols]
                if scale is not None:
                    term = term * scale[p:p + 1, :]
                acc[p] = term if acc[p] is None else acc[p] + term
        for p in range(groups):
            cols = slice(p * LANES, (p + 1) * LANES)
            li[g, :, cols] = jnp.zeros((SPAN, LANES), F32) if acc[p] is None else acc[p]

    for i in range(1, nz):
        @pl.when(z - i >= 0)
        def _():
            recv_r2(i).wait_recv()
    for m in range(zbits):
        @pl.when(bit(z, m))
        def _():
            base = lax.div(z, 1 << m) * (1 << m)
            for q in range(gp):
                row = pl.ds(y * gp + q, 1)
                acc = r2[base - 1, q].astype(F32)
                gap = lt[base - 1, row, :]
                for i in range(2, (1 << m) + 1):
                    acc = acc + r2[base - i, q].astype(F32) * jnp.exp(gap)
                    gap = gap + lt[base - i, row, :]
                zb[m, y * gp + q] = acc.astype(BF16)

    right, left = lax.rem(y + 1, ny), lax.rem(y + ny - 1, ny)
    right_steps = ny // 2
    left_steps = ny - 1 - right_steps

    def hop(m, way, s):
        if way == 0:
            own = lax.rem(y + ny - s, ny)
            goal = right
        else:
            own = lax.rem(y + s, ny)
            goal = left
        part = zb.at[m, pl.ds(own * gp, gp)]
        return remote(part, part, ags.at[0, m, way, s], ags.at[1, m, way, s], to_y(goal))

    def landed(m, way, s):
        own = lax.rem(y + ny - s - 1, ny) if way == 0 else lax.rem(y + s + 1, ny)
        part = zb.at[m, pl.ds(own * gp, gp)]
        return remote(
            part, part, ags.at[0, m, way, s], ags.at[1, m, way, s], to_y(left if way == 0 else right)
        )

    for s in range(right_steps):
        for m in range(zbits):
            @pl.when(bit(z, m))
            def _():
                for way in range(2):
                    if s < (right_steps, left_steps)[way]:
                        if s:
                            landed(m, way, s - 1).wait_recv()
                        hop(m, way, s).start()

    def before_y(lo):
        gap = jnp.zeros((groups, LANES), F32)
        for j in range(ny):
            gap = gap + jnp.where(jnp.logical_and(j >= lo, j < y), tau[j], 0.0)
        return gap

    def before_z(lo):
        gap = jnp.zeros((groups, LANES), F32)
        for j in range(nz):
            gap = gap + jnp.where(jnp.logical_and(j >= lo, j < z), lt[j], 0.0)
        return gap

    def put(slot, part, gap):
        scale = jnp.exp(gap)
        for p in range(groups):
            bks[slot, :, p * LANES:(p + 1) * LANES] = (
                part[p].astype(F32) * scale[p:p + 1, :]
            ).astype(BF16)

    for m in range(ybits):
        @pl.when(bit(y, m))
        def _():
            if m == 0:
                recv_l0().wait_recv()
            else:
                for j in y_round:
                    recv_yb(m, j).wait_recv()
            put(m, yb.at[m], before_y(lax.div(y, 1 << m) * (1 << m)))

        @pl.when(jnp.logical_not(bit(y, m)))
        def _():
            bks[m] = jnp.zeros((STATE, hl * HEAD_DIM), BF16)

    for m in range(zbits):
        @pl.when(bit(z, m))
        def _():
            for way in range(2):
                last = (right_steps, left_steps)[way] - 1
                if last >= 0:
                    landed(m, way, last).wait_recv()
            put(
                ybits + m, zb.at[m],
                before_y(0) + before_z(lax.div(z, 1 << m) * (1 << m)),
            )

        @pl.when(jnp.logical_not(bit(z, m)))
        def _():
            bks[ybits + m] = jnp.zeros((STATE, hl * HEAD_DIM), BF16)

    def cross(g):
        acc = [None] * groups
        for m in range(ybits + zbits):
            v = dot(cr[g], bks[m])
            for p in range(groups):
                cols = slice(p * LANES, (p + 1) * LANES)
                term = we[hbits + m, g, :, cols].astype(F32) * v[:, cols]
                acc[p] = term if acc[p] is None else acc[p] + term
        scale = pg[g]
        for p in range(groups):
            cols = slice(p * LANES, (p + 1) * LANES)
            io[g, :, cols] = (acc[p] * scale[p:p + 1, :] + li[g, :, cols]).astype(BF16)

    for j in heads_round:
        cross(j)
        send_o(j).start()
    cross(hd)
    ir[hd] = io[hd]

    def recv_o(j):
        return remote(io.at[j], ir.at[j], ios.at[0, j], ios.at[1, j], to_head(j))

    def finish(j):
        def one(p, _):
            cols = pl.ds(pl.multiple_of((j * groups + p) * LANES, LANES), LANES)
            part = pl.ds(pl.multiple_of(p * LANES, LANES), LANES)
            m = spread(rows[1], 2 * (j * groups + p))
            out[:, cols] = (o0[:, cols] + m * ir[j, :, part].astype(F32)).astype(BF16)
            return 0

        lax.fori_loop(0, groups, one, 0, unroll=4)

    finish(hd)
    for i in range(nh - 2, -1, -1):
        j = heads_round[i]
        recv_o(j).wait_recv()
        finish(j)

    for j in heads_round:
        send_a(j).wait_send()
        send_b(j).wait_send()
        send_x(j).wait_send()
        send_c(j).wait_send()
        send_o(j).wait_send()
    for j in y_round:
        send_tau(j).wait_send()
        send_r1(j).wait_send()
        for m in range(1, ybits):
            @pl.when(bit(j, m))
            def _():
                send_yb(m, j).wait_send()

    @pl.when(lax.rem(y, 2) == 0)
    def _():
        send_l0().wait_send()

    for i in range(1, nz):
        @pl.when(z + i < nz)
        def _():
            send_lt(i).wait_send()
            send_r2(i).wait_send()
    for s in range(right_steps):
        for m in range(zbits):
            @pl.when(bit(z, m))
            def _():
                for way in range(2):
                    if s < (right_steps, left_steps)[way]:
                        hop(m, way, s).wait_send()


def on_device(nh, ny, nz, token_inputs, state_in, state_out, log_decay, token_codes, table, gain):
    hl = HEADS // nh
    groups = hl // 2
    gp = groups // ny
    wide = hl * HEAD_DIM
    hbits, ybits, zbits = bits_of(nh), bits_of(ny), bits_of(nz)
    nlev = hbits + ybits + zbits
    vm = pltpu.VMEM
    sem = pltpu.SemaphoreType.DMA
    pieces = sum(ny >> (m + 1) for m in range(1, ybits))
    return pl.pallas_call(
        functools.partial(kernel, nh, ny, nz),
        out_shape=jax.ShapeDtypeStruct((SPAN, HEADS * HEAD_DIM), BF16),
        in_specs=[pl.BlockSpec(memory_space=pltpu.VMEM)] * 7,
        out_specs=pl.BlockSpec(memory_space=pltpu.VMEM),
        scratch_shapes=[
            vm((nh, SPAN, wide), BF16),
            vm((nh, SPAN, wide), BF16),
            vm((nh, SPAN, STATE), BF16),
            vm((nh, SPAN, STATE), BF16),
            vm((nh, groups + 8, LANES), F32),
            vm((nh, groups + 8, LANES), F32),
            vm((SPAN, HEADS * HEAD_DIM), F32),
            vm((2, SPAN, LANES), F32),
            vm((nlev, CODES, wide), BF16),
            vm((nh * SPAN, CODES), BF16),
            vm((nlev, nh, SPAN, wide), BF16),
            vm((nh, STATE, wide), F32),
            vm((nh - 1, STATE, wide), BF16),
            vm((nh, SPAN, wide), F32),
            vm((groups, STATE, LANES), BF16),
            vm((ny, gp, STATE, LANES), BF16),
            vm((max(pieces, 1), gp, STATE, LANES), BF16),
            vm((gp, STATE, LANES), BF16),
            vm((nz, gp, STATE, LANES), BF16),
            vm((ybits, groups, STATE, LANES), BF16),
            vm((max(zbits, 1), groups, STATE, LANES), BF16),
            vm((ybits + zbits, STATE, wide), BF16),
            vm((ny, groups, LANES), F32),
            vm((nz, groups, LANES), F32),
            vm((nh, groups, LANES), F32),
            vm((nh, SPAN, wide), BF16),
            vm((nh, SPAN, wide), BF16),
            sem((2, nh)),
            sem((2, nh)),
            sem((2, nh)),
            sem((2, nh)),
            sem((2, ny)),
            sem((2, nz)),
            sem((2, ny)),
            sem((2,)),
            sem((2, max(ybits, 1), ny)),
            sem((2, nz)),
            sem((2, max(zbits, 1), 2, max(ny // 2, 1))),
            sem((2, nh)),
        ],
        compiler_params=pltpu.CompilerParams(
            collective_id=0, has_side_effects=True, vmem_limit_bytes=60 << 20
        ),
    )(
        token_inputs, state_in, state_out, log_decay,
        token_codes.reshape(1, SPAN), table, gain.reshape(1, HEADS),
    )


def solution(mesh, ny=NY):
    nh = mesh.shape["head"]
    nz = mesh.shape["ctx"] // ny
    return jax.shard_map(
        functools.partial(on_device, nh, ny, nz),
        mesh=mesh,
        in_specs=(
            P(("ctx", "head"), None),
            P(("ctx", "head"), None),
            P(("ctx", "head"), None),
            P(("ctx", "head"), None),
            P(("ctx", "head")),
            P(),
            P(),
        ),
        out_specs=P(("ctx", "head"), None),
        check_vma=False,
    )
```

```python
import functools

import jax
import jax.numpy as jnp
from jax import lax
from jax.experimental import pallas as pl
from jax.experimental.pallas import tpu as pltpu
from jax.sharding import PartitionSpec as P

HEADS = 128
HEAD_DIM = 64
STATE = 128
SPAN = 64
LEVELS = 11
CODES = 64
NY = 8
LANES = 128
CHUNKS = 2
SPLIT = 2
TILE = 256
VMEM_LIMIT = 44 << 20
MESH = pl.DeviceIdType.MESH
F32 = jnp.float32
BF16 = jnp.bfloat16


def bits_of(n):
    return n.bit_length() - 1


def dot(a, b):
    return jnp.dot(a, b, preferred_element_type=F32)


def dot_t(a, b):
    return lax.dot_general(a, b, (((0,), (0,)), ((), ())), preferred_element_type=F32)


def iota(shape, dim):
    return lax.broadcasted_iota(jnp.int32, shape, dim)


def spread(v, first):
    idx = first + (iota(v.shape, 1) >> 6)
    return jnp.take_along_axis(v, idx, axis=1, mode="promise_in_bounds")


def kernel(
    nh, ny, nz,
    x, b, c, d, codes, tab, skip, out,
    xc, xr, br, cr, aux, auxr, o0, er, rows, te, oh, we, sg, lbs, li,
    sb, r1, pb, tz, r2, yb, zb, bks, tau, lt, pg, io, ir,
    xs, bs, cs, axs, taus, lts, r1s, l0s, ys, r2s, ags, ios,
):
    hl = HEADS // nh
    groups = hl // 2
    gc = groups // CHUNKS
    units = gc * SPLIT
    up = units // ny
    rp = STATE // SPLIT
    wc = gc * LANES
    tiles = [slice(i, i + TILE) for i in range(0, wc, TILE)]
    hbits, ybits, zbits = bits_of(nh), bits_of(ny), bits_of(nz)
    nlev = hbits + ybits + zbits
    chunks = range(CHUNKS)
    hd = lax.axis_index("head")
    k = lax.axis_index("ctx")
    y = lax.rem(k, ny)
    z = lax.div(k, ny)
    chip, core = lax.div(hd, 2), lax.rem(hd, 2)

    def to_head(j):
        return {"head": j}

    def to_y(j):
        return {"ctx": z * ny + j}

    def to_z(j):
        return {"ctx": j * ny + y}

    def remote(src, dst, send, recv, where):
        return pltpu.make_async_remote_copy(
            src_ref=src, dst_ref=dst, send_sem=send, recv_sem=recv,
            device_id=where, device_id_type=MESH,
        )

    def bit(v, m):
        return lax.rem(lax.div(v, 1 << m), 2) == 1

    hops = sorted(range(1, nh // 2), key=lambda o: -min(o, nh // 2 - o))
    chips_round = [lax.rem(chip + o, nh // 2) for o in hops]
    heads_round = []
    for q in chips_round:
        heads_round += [2 * q + core, 2 * q + 1 - core]
    heads_round.append(2 * chip + 1 - core)
    y_round = [lax.rem(y + i, ny) for i in range(1, ny)]
    z_round = [lax.rem(z + i, nz) for i in range(1, nz)]

    lt[...] = jnp.zeros_like(lt)
    barrier = pltpu.get_barrier_semaphore()
    for j in heads_round:
        pl.semaphore_signal(barrier, inc=1, device_id=to_head(j), device_id_type=MESH)
    for j in y_round:
        pl.semaphore_signal(barrier, inc=1, device_id=to_y(j), device_id_type=MESH)
    for j in z_round:
        pl.semaphore_signal(barrier, inc=1, device_id=to_z(j), device_id_type=MESH)

    lower = iota((SPAN, SPAN), 0) >= iota((SPAN, SPAN), 1)
    run = dot(jnp.where(lower, 1.0, 0.0).astype(BF16), d[...])
    tot = run[SPAN - 1:SPAN, :]
    fac = jnp.exp(tot - run)

    pairs = HEADS // 2
    first = 2 * iota((pairs, LANES), 0) + (iota((pairs, LANES), 1) >> 6)
    tot_pairs = jnp.take_along_axis(
        jnp.broadcast_to(tot, (pairs, LANES)), first, axis=1, mode="promise_in_bounds"
    )
    code_row = codes[...].astype(F32)
    for j in range(nh):
        aux[j, 0:groups, :] = tot_pairs[j * groups:(j + 1) * groups, :]
        aux[j, groups:groups + 8, 0:SPAN] = jnp.broadcast_to(code_row, (8, SPAN))
        aux[j, groups:groups + 8, SPAN:] = jnp.zeros((8, LANES - SPAN), F32)
    auxr[hd] = aux[hd]
    br[hd] = b[...]
    cr[hd] = c[...]

    def carry(ch, j):
        def one(p, _):
            cols = pl.ds(pl.multiple_of(p * LANES, LANES), LANES)
            at = j * groups + ch * gc + p
            src = pl.ds(pl.multiple_of(at * LANES, LANES), LANES)
            m = spread(fac, 2 * at)
            xc[ch, j, :, cols] = (m * x[:, src].astype(F32)).astype(BF16)
            return 0

        lax.fori_loop(0, gc, one, 0, unroll=4)

    def move_x(ch, j, src):
        return remote(
            xc.at[ch, j], xr.at[ch, src], xs.at[0, ch, j], xs.at[1, ch, src], to_head(j)
        )

    def move_b(j, src):
        return remote(b, br.at[src], bs.at[0, j], bs.at[1, src], to_head(j))

    def move_c(j, src):
        return remote(c, cr.at[src], cs.at[0, j], cs.at[1, src], to_head(j))

    def move_a(j, src):
        return remote(aux.at[j], auxr.at[src], axs.at[0, j], axs.at[1, src], to_head(j))

    def move_o(ch, j, src):
        return remote(
            io.at[ch, j], ir.at[ch, src], ios.at[0, ch, j], ios.at[1, ch, src], to_head(j)
        )

    carry(0, heads_round[0])
    pl.semaphore_wait(barrier, (nh - 1) + (ny - 1) + (nz - 1))
    for j in heads_round:
        move_a(j, hd).start()
    for j in heads_round:
        move_b(j, hd).start()
    for ch in chunks:
        for i, j in enumerate(heads_round):
            if i or ch:
                carry(ch, j)
            move_x(ch, j, hd).start()
    for ch in chunks:
        carry(ch, hd)
        xr[ch, hd] = xc[ch, hd]

    for j in heads_round:
        move_a(j, j).wait_recv()
    mine = auxr[0, 0:groups, :]
    for g in range(nh):
        pg[g] = jnp.exp(mine) if g else jnp.ones((groups, LANES), F32)
        if g:
            mine = mine + auxr[g, 0:groups, :]
    tau[y] = mine

    def move_tau(j, src):
        return remote(tau.at[y], tau.at[src], taus.at[0, j], taus.at[1, src], to_y(j))

    for j in y_round:
        move_tau(j, y).start()

    cols0 = iota((LEVELS * HEADS, LANES), 0)
    lane0 = iota((LEVELS * HEADS, LANES), 1)
    tab0 = dot(tab[...], jnp.where(cols0 == lane0 * LEVELS, 1.0, 0.0).astype(BF16)).astype(BF16)
    code_t = jnp.where(
        jnp.broadcast_to(code_row, (CODES, SPAN)) == iota((CODES, SPAN), 0).astype(F32), 1.0, 0.0
    ).astype(BF16)
    w0 = dot_t(code_t, tab0)
    rows[0] = w0 * jnp.exp(run - tot)
    rows[1] = jnp.exp(run)

    per = LANES // hl
    for t in range(-(-nlev // per)):
        lev = 1 + t * per + lane0 // hl
        want = (hd * hl + lax.rem(lane0, hl)) * LEVELS + lev
        picked = dot(tab[...], jnp.where(cols0 == want, 1.0, 0.0).astype(BF16))
        for l in range(t * per, min(nlev, (t + 1) * per)):
            for p in range(groups):
                te[l, :, p * LANES:(p + 1) * LANES] = spread(
                    picked, (l - t * per) * hl + 2 * p
                ).astype(BF16)
    eye = jnp.where(iota((CODES, CODES), 0) == iota((CODES, CODES), 1), 1.0, 0.0).astype(BF16)
    for g in range(nh):
        row = auxr[g, groups:groups + 1, 0:SPAN]
        hot = jnp.where(
            jnp.broadcast_to(row, (CODES, SPAN)) == iota((CODES, SPAN), 0).astype(F32), 1.0, 0.0
        ).astype(BF16)
        oh[g * SPAN:(g + 1) * SPAN, :] = dot_t(hot, eye).astype(BF16)

    scores = lax.dot_general(
        c[...], b[...], (((1,), (1,)), ((), ())), preferred_element_type=F32
    )
    near = jnp.where(lower, scores, 0.0).astype(BF16)
    gain = jnp.broadcast_to(skip[...], (SPAN, LANES))

    def level0(j, _):
        for ch in chunks:
            v = dot(near, xc[ch, j])
            for p in range(gc):
                at = j * groups + ch * gc + p
                cols = pl.ds(pl.multiple_of(at * LANES, LANES), LANES)
                o0[:, cols] = (
                    spread(rows[0], 2 * at) * v[:, p * LANES:(p + 1) * LANES]
                    + spread(gain, 2 * at) * x[:, cols].astype(F32)
                )
        return 0

    lax.fori_loop(0, nh, level0, 0)

    for j in y_round:
        move_tau(j, j).wait_recv()
    line = tau[0]
    for j in range(1, ny):
        line = line + tau[j]
    lt[z] = line

    def send_lt(i):
        return remote(lt.at[z], lt.at[z], lts.at[0, z + i], lts.at[1, z], to_z(z + i))

    def recv_lt(i):
        return remote(lt.at[z], lt.at[z - i], lts.at[0, z], lts.at[1, z - i], to_z(z - i))

    for i in range(1, nz):
        @pl.when(z + i < nz)
        def _():
            send_lt(i).start()

    offs = [0]
    for m in range(hbits):
        offs.append(offs[-1] + (nh >> (m + 1)))

    def fold(ch):
        def one(p, _):
            cols = pl.ds(pl.multiple_of(p * LANES, LANES), LANES)
            cur = [sg[g, :, cols] for g in range(nh)]
            dec = [auxr[g, pl.ds(ch * gc + p, 1), :] for g in range(nh)]
            for m in range(hbits):
                new, new_dec = [], []
                for i in range(len(cur) // 2):
                    lbs[ch, offs[m] + i, :, cols] = cur[2 * i].astype(BF16)
                    new.append(cur[2 * i] * jnp.exp(dec[2 * i + 1]) + cur[2 * i + 1])
                    new_dec.append(dec[2 * i] + dec[2 * i + 1])
                cur, dec = new, new_dec
            for r in range(SPLIT):
                sb[ch, p * SPLIT + r] = cur[0][r * rp:(r + 1) * rp].astype(BF16)
            return 0

        lax.fori_loop(0, gc, one, 0)

    def move_r1(ch, j, src):
        return remote(
            sb.at[ch, pl.ds(j * up, up)], r1.at[ch, src],
            r1s.at[0, ch, j], r1s.at[1, ch, src], to_y(j),
        )

    def move_l0(ch, j):
        return remote(sb.at[ch], yb.at[ch, 0], l0s.at[0, ch], l0s.at[1, ch], to_y(j))

    for ch in chunks:
        sg[hd] = dot_t(br[hd], xr[ch, hd])
        for j in reversed(heads_round):
            if ch == 0:
                move_b(j, j).wait_recv()
            move_x(ch, j, j).wait_recv()
            sg[j] = dot_t(br[j], xr[ch, j])
        fold(ch)
        for j in y_round:
            move_r1(ch, j, y).start()

        @pl.when(lax.rem(y, 2) == 0)
        def _():
            move_l0(ch, y + 1).start()

        for q in range(up):
            r1[ch, y, q] = sb[ch, y * up + q]
    for j in heads_round:
        move_c(j, hd).start()

    def weigh(l, cols, g0, g1):
        w = dot(oh[g0 * SPAN:g1 * SPAN, :], te[l, :, cols]).astype(BF16)
        for t in range(g0 // 2, g1 // 2):
            we[l, t, :, cols] = w[(2 * t - g0) * SPAN:(2 * t + 2 - g0) * SPAN]

    for l in range(nlev):
        for i in range(0, groups * LANES, TILE):
            if l < hbits and l > 0:
                for g in range(2 << l >> 1, nh, 2 << l):
                    weigh(l, slice(i, i + TILE), g, g + (1 << l))
            else:
                weigh(l, slice(i, i + TILE), 0, nh)

    for i in range(1, nz):
        @pl.when(z - i >= 0)
        def _():
            recv_lt(i).wait_recv()

    yoffs = [0]
    for m in range(1, ybits):
        yoffs.append(yoffs[-1] + (ny >> (m + 1)))

    def row_of(ch, q):
        return pl.ds(ch * gc + lax.div(y * up + q, SPLIT), 1)

    def send_r2(ch, i):
        return remote(
            tz.at[ch], r2.at[ch, z], r2s.at[0, ch, z + i], r2s.at[1, ch, z], to_z(z + i)
        )

    def recv_r2(ch, i):
        return remote(
            tz.at[ch], r2.at[ch, z - i], r2s.at[0, ch, z], r2s.at[1, ch, z - i], to_z(z - i)
        )

    def move_yb(ch, m, j, src):
        return remote(
            pb.at[ch, yoffs[m - 1] + lax.div(j, 2 << m)], yb.at[ch, m, pl.ds(src * up, up)],
            ys.at[0, ch, m, j], ys.at[1, ch, m, src], to_y(j),
        )

    for ch in chunks:
        for j in y_round:
            move_r1(ch, j, j).wait_recv()
        for q in range(up):
            cur = [r1[ch, j, q].astype(F32) for j in range(ny)]
            dec = [tau[j, row_of(ch, q), :] for j in range(ny)]
            for m in range(ybits):
                new, new_dec = [], []
                for i in range(len(cur) // 2):
                    if m:
                        pb[ch, yoffs[m - 1] + i, q] = cur[2 * i].astype(BF16)
                    new.append(cur[2 * i] * jnp.exp(dec[2 * i + 1]) + cur[2 * i + 1])
                    new_dec.append(dec[2 * i] + dec[2 * i + 1])
                cur, dec = new, new_dec
            r2[ch, z, q] = cur[0].astype(BF16)
            tz[ch, q] = cur[0].astype(BF16)
        for i in range(1, nz):
            @pl.when(z + i < nz)
            def _():
                send_r2(ch, i).start()
        for m in range(1, ybits):
            for j in y_round:
                @pl.when(bit(j, m))
                def _():
                    move_yb(ch, m, j, y).start()

            @pl.when(bit(y, m))
            def _():
                for q in range(up):
                    yb[ch, m, y * up + q] = pb[ch, yoffs[m - 1] + lax.div(y, 2 << m), q]

    for j in heads_round:
        move_c(j, j).wait_recv()

    def cpair(t):
        return cr[pl.ds(2 * t, 2)].reshape(2 * SPAN, STATE)

    def scaled(v, row0, row1):
        return jnp.concatenate([v[:SPAN] * row0, v[SPAN:] * row1], axis=0)

    def gap_rows(lo, g):
        gap = jnp.zeros((groups, LANES), F32)
        for before in range(lo, g):
            gap = gap + auxr[before, 0:groups, :]
        return jnp.exp(gap)

    def wide_rows(tile, ch, cols):
        at = [ch * gc + i // LANES for i in range(cols.start, cols.stop, LANES)]
        return jnp.concatenate([tile[i:i + 1, :] for i in at], axis=1)

    def inner(ch):
        for t in range(nh // 2):
            cp = cpair(t)
            for cols in tiles:
                full = slice(ch * wc + cols.start, ch * wc + cols.stop)
                v = dot(cp[SPAN:], lbs[ch, t, :, cols]) * we[0, t, SPAN:, full].astype(F32)
                acc = None
                for m in range(1, hbits):
                    if not 2 * t >> m & 1:
                        continue
                    lo = 2 * t >> m << m
                    term = we[m, t, :, full].astype(F32) * dot(
                        cp, lbs[ch, offs[m] + (2 * t >> (m + 1)), :, cols]
                    )
                    term = scaled(
                        term,
                        wide_rows(gap_rows(lo, 2 * t), ch, cols),
                        wide_rows(gap_rows(lo, 2 * t + 1), ch, cols),
                    )
                    acc = term if acc is None else acc + term
                if acc is None:
                    li[t, :SPAN, full] = jnp.zeros((SPAN, TILE), F32)
                    li[t, SPAN:, full] = v
                else:
                    li[t, :SPAN, full] = acc[:SPAN]
                    li[t, SPAN:, full] = acc[SPAN:] + v

    for ch in chunks:
        inner(ch)

    right, left = lax.rem(y + 1, ny), lax.rem(y + ny - 1, ny)
    steps = (ny // 2, ny - 1 - ny // 2)

    def hop(ch, m, way, s):
        own = lax.rem(y + ny - s, ny) if way == 0 else lax.rem(y + s, ny)
        part = zb.at[ch, m, pl.ds(own * up, up)]
        return remote(
            part, part, ags.at[0, ch, m, way, s], ags.at[1, ch, m, way, s],
            to_y(right if way == 0 else left),
        )

    def landed(ch, m, way, s):
        own = lax.rem(y + ny - s - 1, ny) if way == 0 else lax.rem(y + s + 1, ny)
        part = zb.at[ch, m, pl.ds(own * up, up)]
        return remote(
            part, part, ags.at[0, ch, m, way, s], ags.at[1, ch, m, way, s],
            to_y(left if way == 0 else right),
        )

    def pass_on(ch, s):
        for m in range(zbits):
            @pl.when(bit(z, m))
            def _():
                for way in range(2):
                    if s < steps[way]:
                        if s:
                            landed(ch, m, way, s - 1).wait_recv()
                        hop(ch, m, way, s).start()

    def before_y(lo):
        gap = jnp.zeros((groups, LANES), F32)
        for j in range(ny):
            gap = gap + jnp.where(jnp.logical_and(j >= lo, j < y), tau[j], 0.0)
        return gap

    def before_z(lo):
        gap = jnp.zeros((groups, LANES), F32)
        for j in range(nz):
            gap = gap + jnp.where(jnp.logical_and(j >= lo, j < z), lt[j], 0.0)
        return gap

    def put(ch, slot, part, gap):
        scale = jnp.exp(gap)
        for p in range(gc):
            for r in range(SPLIT):
                bks[ch, slot, r * rp:(r + 1) * rp, p * LANES:(p + 1) * LANES] = (
                    part[p * SPLIT + r].astype(F32) * scale[ch * gc + p:ch * gc + p + 1, :]
                ).astype(BF16)

    def put_y(ch):
        for m in range(ybits):
            @pl.when(bit(y, m))
            def _():
                if m == 0:
                    move_l0(ch, y - 1).wait_recv()
                else:
                    for j in y_round:
                        move_yb(ch, m, j, j).wait_recv()
                put(ch, m, yb.at[ch, m], before_y(lax.div(y, 1 << m) * (1 << m)))

            @pl.when(jnp.logical_not(bit(y, m)))
            def _():
                bks[ch, m] = jnp.zeros((STATE, wc), BF16)

    def put_z(ch):
        for m in range(zbits):
            @pl.when(bit(z, m))
            def _():
                for way in range(2):
                    if steps[way]:
                        landed(ch, m, way, steps[way] - 1).wait_recv()
                put(
                    ch, ybits + m, zb.at[ch, m],
                    before_y(0) + before_z(lax.div(z, 1 << m) * (1 << m)),
                )

            @pl.when(jnp.logical_not(bit(z, m)))
            def _():
                bks[ch, ybits + m] = jnp.zeros((STATE, wc), BF16)

    def cross(ch, t, cols, levels):
        full = slice(ch * wc + cols.start, ch * wc + cols.stop)
        cp = cpair(t)
        acc = None
        for m in levels:
            term = we[hbits + m, t, :, full].astype(F32) * dot(cp, bks[ch, m, :, cols])
            acc = term if acc is None else acc + term
        acc = scaled(
            acc, wide_rows(pg[2 * t], ch, cols), wide_rows(pg[2 * t + 1], ch, cols)
        )
        return acc + li[t, :, full]

    def cross_y(ch):
        def one(t, _):
            for cols in tiles:
                full = slice(ch * wc + cols.start, ch * wc + cols.stop)
                li[t, :, full] = cross(ch, t, cols, range(ybits))
            return 0

        lax.fori_loop(0, nh // 2, one, 0)

    def cross_z(ch, t):
        for cols in tiles:
            v = cross(ch, t, cols, range(ybits, ybits + zbits)).astype(BF16)
            io[ch, 2 * t, :, cols] = v[:SPAN]
            io[ch, 2 * t + 1, :, cols] = v[SPAN:]

    def return_rows():
        def one(p, _):
            cols = pl.ds(pl.multiple_of(p * LANES, LANES), LANES)
            er[:, cols] = spread(rows[1], 2 * p)
            return 0

        lax.fori_loop(0, HEADS // 2, one, 0, unroll=4)

    for ch in chunks:
        for i in range(1, nz):
            @pl.when(z - i >= 0)
            def _():
                recv_r2(ch, i).wait_recv()
        for m in range(zbits):
            @pl.when(bit(z, m))
            def _():
                base = lax.div(z, 1 << m) * (1 << m)
                for q in range(up):
                    acc = r2[ch, base - 1, q].astype(F32)
                    gap = lt[base - 1, row_of(ch, q), :]
                    for i in range(2, (1 << m) + 1):
                        acc = acc + r2[ch, base - i, q].astype(F32) * jnp.exp(gap)
                        gap = gap + lt[base - i, row_of(ch, q), :]
                    zb[ch, m, y * up + q] = acc.astype(BF16)
        pass_on(ch, 0)
    return_rows()
    for s in range(1, steps[0]):
        for ch in chunks:
            pass_on(ch, s)
        if s - 1 < CHUNKS:
            put_y(s - 1)
            cross_y(s - 1)
    for ch in range(max(steps[0] - 1, 0), CHUNKS):
        put_y(ch)
        cross_y(ch)

    for ch in chunks:
        put_z(ch)
        for i, t in enumerate(chips_round):
            cross_z(ch, t)
            for j in heads_round[2 * i:2 * i + 2]:
                move_o(ch, j, hd).start()
        cross_z(ch, chip)
        move_o(ch, heads_round[-1], hd).start()
        ir[ch, hd] = io[ch, hd]

    def finish(ch, j):
        def one(p, _):
            at = j * groups + ch * gc + p
            cols = pl.ds(pl.multiple_of(at * LANES, LANES), LANES)
            part = pl.ds(pl.multiple_of(p * LANES, LANES), LANES)
            out[:, cols] = (
                o0[:, cols] + er[:, cols] * ir[ch, j, :, part].astype(F32)
            ).astype(BF16)
            return 0

        lax.fori_loop(0, gc, one, 0, unroll=4)

    for ch in chunks:
        finish(ch, hd)
        for j in heads_round[::-1]:
            move_o(ch, j, j).wait_recv()
            finish(ch, j)

    for j in heads_round:
        move_a(j, hd).wait_send()
        move_b(j, hd).wait_send()
        move_c(j, hd).wait_send()
        for ch in chunks:
            move_x(ch, j, hd).wait_send()
            move_o(ch, j, hd).wait_send()
    for j in y_round:
        move_tau(j, y).wait_send()
        for ch in chunks:
            move_r1(ch, j, y).wait_send()
        for m in range(1, ybits):
            @pl.when(bit(j, m))
            def _():
                for ch in chunks:
                    move_yb(ch, m, j, y).wait_send()

    @pl.when(lax.rem(y, 2) == 0)
    def _():
        for ch in chunks:
            move_l0(ch, y + 1).wait_send()

    for i in range(1, nz):
        @pl.when(z + i < nz)
        def _():
            send_lt(i).wait_send()
            for ch in chunks:
                send_r2(ch, i).wait_send()
    for s in range(steps[0]):
        for m in range(zbits):
            @pl.when(bit(z, m))
            def _():
                for ch in chunks:
                    for way in range(2):
                        if s < steps[way]:
                            hop(ch, m, way, s).wait_send()


def on_device(nh, ny, nz, token_inputs, state_in, state_out, log_decay, token_codes, table, gain):
    hl = HEADS // nh
    groups = hl // 2
    gc = groups // CHUNKS
    units = gc * SPLIT
    up = units // ny
    rp = STATE // SPLIT
    wide = hl * HEAD_DIM
    wc = wide // CHUNKS
    hbits, ybits, zbits = bits_of(nh), bits_of(ny), bits_of(nz)
    nlev = hbits + ybits + zbits
    vm = pltpu.VMEM
    sem = pltpu.SemaphoreType.DMA
    pieces = max(sum(ny >> (m + 1) for m in range(1, ybits)), 1)
    nc = CHUNKS
    zb = max(zbits, 1)
    return pl.pallas_call(
        functools.partial(kernel, nh, ny, nz),
        out_shape=jax.ShapeDtypeStruct((SPAN, HEADS * HEAD_DIM), BF16),
        in_specs=[pl.BlockSpec(memory_space=pltpu.VMEM)] * 7,
        out_specs=pl.BlockSpec(memory_space=pltpu.VMEM),
        scratch_shapes=[
            vm((nc, nh, SPAN, wc), BF16),
            vm((nc, nh, SPAN, wc), BF16),
            vm((nh, SPAN, STATE), BF16),
            vm((nh, SPAN, STATE), BF16),
            vm((nh, groups + 8, LANES), F32),
            vm((nh, groups + 8, LANES), F32),
            vm((SPAN, HEADS * HEAD_DIM), F32),
            vm((SPAN, HEADS * HEAD_DIM), F32),
            vm((2, SPAN, LANES), F32),
            vm((nlev, CODES, wide), BF16),
            vm((nh * SPAN, CODES), BF16),
            vm((nlev, nh // 2, 2 * SPAN, wide), BF16),
            vm((nh, STATE, wc), F32),
            vm((nc, nh - 1, STATE, wc), BF16),
            vm((nh // 2, 2 * SPAN, wide), F32),
            vm((nc, units, rp, LANES), BF16),
            vm((nc, ny, up, rp, LANES), BF16),
            vm((nc, pieces, up, rp, LANES), BF16),
            vm((nc, up, rp, LANES), BF16),
            vm((nc, nz, up, rp, LANES), BF16),
            vm((nc, ybits, units, rp, LANES), BF16),
            vm((nc, zb, units, rp, LANES), BF16),
            vm((nc, ybits + zbits, STATE, wc), BF16),
            vm((ny, groups, LANES), F32),
            vm((nz, groups, LANES), F32),
            vm((nh, groups, LANES), F32),
            vm((nc, nh, SPAN, wc), BF16),
            vm((nc, nh, SPAN, wc), BF16),
            sem((2, nc, nh)),
            sem((2, nh)),
            sem((2, nh)),
            sem((2, nh)),
            sem((2, ny)),
            sem((2, nz)),
            sem((2, nc, ny)),
            sem((2, nc)),
            sem((2, nc, max(ybits, 1), ny)),
            sem((2, nc, nz)),
            sem((2, nc, zb, 2, max(ny // 2, 1))),
            sem((2, nc, nh)),
        ],
        compiler_params=pltpu.CompilerParams(
            collective_id=0, has_side_effects=True, vmem_limit_bytes=VMEM_LIMIT
        ),
    )(
        token_inputs, state_in, state_out, log_decay,
        token_codes.reshape(1, SPAN), table, gain.reshape(1, HEADS),
    )


def solution(mesh, ny=NY):
    nh = mesh.shape["head"]
    nz = mesh.shape["ctx"] // ny
    return jax.shard_map(
        functools.partial(on_device, nh, ny, nz),
        mesh=mesh,
        in_specs=(
            P(("ctx", "head"), None),
            P(("ctx", "head"), None),
            P(("ctx", "head"), None),
            P(("ctx", "head"), None),
            P(("ctx", "head")),
            P(),
            P(),
        ),
        out_specs=P(("ctx", "head"), None),
        check_vma=False,
    )
```

```python
import functools

import jax
import jax.numpy as jnp
from jax import lax
from jax.experimental import pallas as pl
from jax.experimental.pallas import tpu as pltpu
from jax.sharding import PartitionSpec as P

HEADS = 128
HEAD_DIM = 64
STATE = 128
SPAN = 64
LEVELS = 11
CODES = 64
NY = 8
LANES = 128
CHUNKS = 2
SPLIT = 2
TILE = 256
VMEM_LIMIT = 44 << 20
MESH = pl.DeviceIdType.MESH
F32 = jnp.float32
BF16 = jnp.bfloat16


def bits_of(n):
    return n.bit_length() - 1


def dot(a, b):
    return jnp.dot(a, b, preferred_element_type=F32)


def dot_t(a, b):
    return lax.dot_general(a, b, (((0,), (0,)), ((), ())), preferred_element_type=F32)


def iota(shape, dim):
    return lax.broadcasted_iota(jnp.int32, shape, dim)


def spread(v, first):
    idx = first + (iota(v.shape, 1) >> 6)
    return jnp.take_along_axis(v, idx, axis=1, mode="promise_in_bounds")


def kernel(
    nh, ny, nz,
    x_in, b_in, c_in, d_in, codes_in, tab_in, skip_in, out,
    x, d, codes, tab, skip,
    xc, xr, br, cr, aux, auxr, o0, er, rows, te, oh, we, sg, lbs, li,
    sb, r1, pb, tz, r2, yb, zb, bks, tau, lt, pg, io, ir,
    ins, xs, bs, cs, axs, taus, lts, r1s, l0s, ys, r2s, ags, ios,
):
    hl = HEADS // nh
    groups = hl // 2
    gc = groups // CHUNKS
    units = gc * SPLIT
    up = units // ny
    rp = STATE // SPLIT
    wc = gc * LANES
    tiles = [slice(i, i + TILE) for i in range(0, wc, TILE)]
    hbits, ybits, zbits = bits_of(nh), bits_of(ny), bits_of(nz)
    nlev = hbits + ybits + zbits
    chunks = range(CHUNKS)
    hd = lax.axis_index("head")
    k = lax.axis_index("ctx")
    y = lax.rem(k, ny)
    z = lax.div(k, ny)
    chip, core = lax.div(hd, 2), lax.rem(hd, 2)

    def to_head(j):
        return {"head": j}

    def to_y(j):
        return {"ctx": z * ny + j}

    def to_z(j):
        return {"ctx": j * ny + y}

    def remote(src, dst, send, recv, where):
        return pltpu.make_async_remote_copy(
            src_ref=src, dst_ref=dst, send_sem=send, recv_sem=recv,
            device_id=where, device_id_type=MESH,
        )

    def bit(v, m):
        return lax.rem(lax.div(v, 1 << m), 2) == 1

    hops = sorted(range(1, nh // 2), key=lambda o: -min(o, nh // 2 - o))
    chips_round = [lax.rem(chip + o, nh // 2) for o in hops]
    heads_round = []
    for q in chips_round:
        heads_round += [2 * q + core, 2 * q + 1 - core]
    heads_round.append(2 * chip + 1 - core)
    y_round = [lax.rem(y + i, ny) for i in range(1, ny)]
    z_round = [lax.rem(z + i, nz) for i in range(1, nz)]

    lt[...] = jnp.zeros_like(lt)
    barrier = pltpu.get_barrier_semaphore()
    for j in heads_round:
        pl.semaphore_signal(barrier, inc=1, device_id=to_head(j), device_id_type=MESH)
    for j in y_round:
        pl.semaphore_signal(barrier, inc=1, device_id=to_y(j), device_id_type=MESH)
    for j in z_round:
        pl.semaphore_signal(barrier, inc=1, device_id=to_z(j), device_id_type=MESH)

    loads = [
        pltpu.make_async_copy(src, dst, ins.at[i])
        for i, (src, dst) in enumerate((
            (d_in, d), (x_in, x), (b_in, br.at[hd]), (c_in, cr.at[hd]),
            (codes_in, codes), (tab_in, tab), (skip_in, skip),
        ))
    ]
    for load in loads:
        load.start()
    b, c = br.at[hd], cr.at[hd]

    loads[0].wait()
    lower = iota((SPAN, SPAN), 0) >= iota((SPAN, SPAN), 1)
    run = dot(jnp.where(lower, 1.0, 0.0).astype(BF16), d[...])
    tot = run[SPAN - 1:SPAN, :]
    fac = jnp.exp(tot - run)

    def carry(ch, j):
        def one(p, _):
            cols = pl.ds(pl.multiple_of(p * LANES, LANES), LANES)
            at = j * groups + ch * gc + p
            src = pl.ds(pl.multiple_of(at * LANES, LANES), LANES)
            m = spread(fac, 2 * at)
            xc[ch, j, :, cols] = (m * x[:, src].astype(F32)).astype(BF16)
            return 0

        lax.fori_loop(0, gc, one, 0, unroll=4)

    def move_x(ch, j, src):
        return remote(
            xc.at[ch, j], xr.at[ch, src], xs.at[0, ch, j], xs.at[1, ch, src], to_head(j)
        )

    def move_b(j, src):
        return remote(b, br.at[src], bs.at[0, j], bs.at[1, src], to_head(j))

    def move_c(j, src):
        return remote(c, cr.at[src], cs.at[0, j], cs.at[1, src], to_head(j))

    def move_a(j, src):
        return remote(aux.at[j], auxr.at[src], axs.at[0, j], axs.at[1, src], to_head(j))

    def move_o(ch, j, src):
        return remote(
            io.at[ch, j], ir.at[ch, src], ios.at[0, ch, j], ios.at[1, ch, src], to_head(j)
        )

    def share_aux():
        pairs = HEADS // 2
        first = 2 * iota((pairs, LANES), 0) + (iota((pairs, LANES), 1) >> 6)
        tot_pairs = jnp.take_along_axis(
            jnp.broadcast_to(tot, (pairs, LANES)), first, axis=1, mode="promise_in_bounds"
        )
        code_row = codes[...].astype(F32)
        for j in range(nh):
            aux[j, 0:groups, :] = tot_pairs[j * groups:(j + 1) * groups, :]
            aux[j, groups:groups + 8, 0:SPAN] = jnp.broadcast_to(code_row, (8, SPAN))
            aux[j, groups:groups + 8, SPAN:] = jnp.zeros((8, LANES - SPAN), F32)
        auxr[hd] = aux[hd]
        for j in heads_round:
            move_a(j, hd).start()

    for load in loads[1:]:
        load.wait()
    carry(0, heads_round[0])
    pl.semaphore_wait(barrier, (nh - 1) + (ny - 1) + (nz - 1))
    for ch in chunks:
        for i, j in enumerate(heads_round):
            if i or ch:
                carry(ch, j)
            move_x(ch, j, hd).start()
            if ch == 0:
                move_b(j, hd).start()
        if ch == 0:
            share_aux()
    for ch in chunks:
        carry(ch, hd)
        xr[ch, hd] = xc[ch, hd]

    for j in heads_round:
        move_a(j, j).wait_recv()
    mine = auxr[0, 0:groups, :]
    for g in range(nh):
        pg[g] = jnp.exp(mine) if g else jnp.ones((groups, LANES), F32)
        if g:
            mine = mine + auxr[g, 0:groups, :]
    tau[y] = mine

    def move_tau(j, src):
        return remote(tau.at[y], tau.at[src], taus.at[0, j], taus.at[1, src], to_y(j))

    for j in y_round:
        move_tau(j, y).start()

    cols0 = iota((LEVELS * HEADS, LANES), 0)
    lane0 = iota((LEVELS * HEADS, LANES), 1)
    tab0 = dot(tab[...], jnp.where(cols0 == lane0 * LEVELS, 1.0, 0.0).astype(BF16)).astype(BF16)
    code_row = codes[...].astype(F32)
    code_t = jnp.where(
        jnp.broadcast_to(code_row, (CODES, SPAN)) == iota((CODES, SPAN), 0).astype(F32), 1.0, 0.0
    ).astype(BF16)
    w0 = dot_t(code_t, tab0)
    rows[0] = w0 * jnp.exp(run - tot)
    rows[1] = jnp.exp(run)

    per = LANES // hl
    for t in range(-(-nlev // per)):
        lev = 1 + t * per + lane0 // hl
        want = (hd * hl + lax.rem(lane0, hl)) * LEVELS + lev
        picked = dot(tab[...], jnp.where(cols0 == want, 1.0, 0.0).astype(BF16))
        for l in range(t * per, min(nlev, (t + 1) * per)):
            for p in range(groups):
                te[l, :, p * LANES:(p + 1) * LANES] = spread(
                    picked, (l - t * per) * hl + 2 * p
                ).astype(BF16)
    eye = jnp.where(iota((CODES, CODES), 0) == iota((CODES, CODES), 1), 1.0, 0.0).astype(BF16)
    for g in range(nh):
        row = auxr[g, groups:groups + 1, 0:SPAN]
        hot = jnp.where(
            jnp.broadcast_to(row, (CODES, SPAN)) == iota((CODES, SPAN), 0).astype(F32), 1.0, 0.0
        ).astype(BF16)
        oh[g * SPAN:(g + 1) * SPAN, :] = dot_t(hot, eye).astype(BF16)

    scores = lax.dot_general(
        c[...], b[...], (((1,), (1,)), ((), ())), preferred_element_type=F32
    )
    near = jnp.where(lower, scores, 0.0).astype(BF16)
    gain = jnp.broadcast_to(skip[...], (SPAN, LANES))

    def level0(j, _):
        for ch in chunks:
            v = dot(near, xc[ch, j])
            for p in range(gc):
                at = j * groups + ch * gc + p
                cols = pl.ds(pl.multiple_of(at * LANES, LANES), LANES)
                o0[:, cols] = (
                    spread(rows[0], 2 * at) * v[:, p * LANES:(p + 1) * LANES]
                    + spread(gain, 2 * at) * x[:, cols].astype(F32)
                )
        return 0

    lax.fori_loop(0, nh, level0, 0)

    for j in y_round:
        move_tau(j, j).wait_recv()
    line = tau[0]
    for j in range(1, ny):
        line = line + tau[j]
    lt[z] = line

    def send_lt(i):
        return remote(lt.at[z], lt.at[z], lts.at[0, z + i], lts.at[1, z], to_z(z + i))

    def recv_lt(i):
        return remote(lt.at[z], lt.at[z - i], lts.at[0, z], lts.at[1, z - i], to_z(z - i))

    for i in range(1, nz):
        @pl.when(z + i < nz)
        def _():
            send_lt(i).start()

    def weigh(l, cols, g0, g1):
        w = dot(oh[g0 * SPAN:g1 * SPAN, :], te[l, :, cols]).astype(BF16)
        for t in range(g0 // 2, g1 // 2):
            we[l, t, :, cols] = w[(2 * t - g0) * SPAN:(2 * t + 2 - g0) * SPAN]

    for l in range(nlev):
        for i in range(0, groups * LANES, TILE):
            if l < hbits and l > 0:
                for g in range(2 << l >> 1, nh, 2 << l):
                    weigh(l, slice(i, i + TILE), g, g + (1 << l))
            else:
                weigh(l, slice(i, i + TILE), 0, nh)

    offs = [0]
    for m in range(hbits):
        offs.append(offs[-1] + (nh >> (m + 1)))

    def fold(ch):
        def one(p, _):
            cols = pl.ds(pl.multiple_of(p * LANES, LANES), LANES)
            cur = [sg[g, :, cols] for g in range(nh)]
            dec = [auxr[g, pl.ds(ch * gc + p, 1), :] for g in range(nh)]
            for m in range(hbits):
                new, new_dec = [], []
                for i in range(len(cur) // 2):
                    lbs[ch, offs[m] + i, :, cols] = cur[2 * i].astype(BF16)
                    new.append(cur[2 * i] * jnp.exp(dec[2 * i + 1]) + cur[2 * i + 1])
                    new_dec.append(dec[2 * i] + dec[2 * i + 1])
                cur, dec = new, new_dec
            for r in range(SPLIT):
                sb[ch, p * SPLIT + r] = cur[0][r * rp:(r + 1) * rp].astype(BF16)
            return 0

        lax.fori_loop(0, gc, one, 0)

    def move_r1(ch, j, src):
        return remote(
            sb.at[ch, pl.ds(j * up, up)], r1.at[ch, src],
            r1s.at[0, ch, j], r1s.at[1, ch, src], to_y(j),
        )

    def move_l0(ch, j):
        return remote(sb.at[ch], yb.at[ch, 0], l0s.at[0, ch], l0s.at[1, ch], to_y(j))

    for ch in chunks:
        sg[hd] = dot_t(br[hd], xr[ch, hd])
        for j in reversed(heads_round):
            if ch == 0:
                move_b(j, j).wait_recv()
            move_x(ch, j, j).wait_recv()
            sg[j] = dot_t(br[j], xr[ch, j])
        fold(ch)
        for j in y_round:
            move_r1(ch, j, y).start()

        @pl.when(lax.rem(y, 2) == 0)
        def _():
            move_l0(ch, y + 1).start()

        for q in range(up):
            r1[ch, y, q] = sb[ch, y * up + q]
    for j in heads_round:
        move_c(j, hd).start()

    for i in range(1, nz):
        @pl.when(z - i >= 0)
        def _():
            recv_lt(i).wait_recv()

    yoffs = [0]
    for m in range(1, ybits):
        yoffs.append(yoffs[-1] + (ny >> (m + 1)))

    def row_of(ch, q):
        return pl.ds(ch * gc + lax.div(y * up + q, SPLIT), 1)

    def send_r2(ch, i):
        return remote(
            tz.at[ch], r2.at[ch, z], r2s.at[0, ch, z + i], r2s.at[1, ch, z], to_z(z + i)
        )

    def recv_r2(ch, i):
        return remote(
            tz.at[ch], r2.at[ch, z - i], r2s.at[0, ch, z], r2s.at[1, ch, z - i], to_z(z - i)
        )

    def move_yb(ch, m, j, src):
        return remote(
            pb.at[ch, yoffs[m - 1] + lax.div(j, 2 << m)], yb.at[ch, m, pl.ds(src * up, up)],
            ys.at[0, ch, m, j], ys.at[1, ch, m, src], to_y(j),
        )

    def line_sums(ch):
        for j in y_round:
            move_r1(ch, j, j).wait_recv()
        for q in range(up):
            cur = [r1[ch, j, q].astype(F32) for j in range(ny)]
            dec = [tau[j, row_of(ch, q), :] for j in range(ny)]
            for m in range(ybits):
                new, new_dec = [], []
                for i in range(len(cur) // 2):
                    if m:
                        pb[ch, yoffs[m - 1] + i, q] = cur[2 * i].astype(BF16)
                    new.append(cur[2 * i] * jnp.exp(dec[2 * i + 1]) + cur[2 * i + 1])
                    new_dec.append(dec[2 * i] + dec[2 * i + 1])
                cur, dec = new, new_dec
            r2[ch, z, q] = cur[0].astype(BF16)
            tz[ch, q] = cur[0].astype(BF16)
        for i in range(1, nz):
            @pl.when(z + i < nz)
            def _():
                send_r2(ch, i).start()
        for m in range(1, ybits):
            for j in y_round:
                @pl.when(bit(j, m))
                def _():
                    move_yb(ch, m, j, y).start()

            @pl.when(bit(y, m))
            def _():
                for q in range(up):
                    yb[ch, m, y * up + q] = pb[ch, yoffs[m - 1] + lax.div(y, 2 << m), q]

    line_sums(0)

    for j in heads_round:
        move_c(j, j).wait_recv()

    def cpair(t):
        return cr[pl.ds(2 * t, 2)].reshape(2 * SPAN, STATE)

    def scaled(v, row0, row1):
        return jnp.concatenate([v[:SPAN] * row0, v[SPAN:] * row1], axis=0)

    def gap_rows(lo, g):
        gap = jnp.zeros((groups, LANES), F32)
        for before in range(lo, g):
            gap = gap + auxr[before, 0:groups, :]
        return jnp.exp(gap)

    def wide_rows(tile, ch, cols):
        at = [ch * gc + i // LANES for i in range(cols.start, cols.stop, LANES)]
        return jnp.concatenate([tile[i:i + 1, :] for i in at], axis=1)

    def inner(ch):
        for t in range(nh // 2):
            cp = cpair(t)
            for cols in tiles:
                full = slice(ch * wc + cols.start, ch * wc + cols.stop)
                v = dot(cp[SPAN:], lbs[ch, t, :, cols]) * we[0, t, SPAN:, full].astype(F32)
                acc = None
                for m in range(1, hbits):
                    if not 2 * t >> m & 1:
                        continue
                    lo = 2 * t >> m << m
                    term = we[m, t, :, full].astype(F32) * dot(
                        cp, lbs[ch, offs[m] + (2 * t >> (m + 1)), :, cols]
                    )
                    term = scaled(
                        term,
                        wide_rows(gap_rows(lo, 2 * t), ch, cols),
                        wide_rows(gap_rows(lo, 2 * t + 1), ch, cols),
                    )
                    acc = term if acc is None else acc + term
                if acc is None:
                    li[t, :SPAN, full] = jnp.zeros((SPAN, TILE), F32)
                    li[t, SPAN:, full] = v
                else:
                    li[t, :SPAN, full] = acc[:SPAN]
                    li[t, SPAN:, full] = acc[SPAN:] + v

    for ch in chunks:
        inner(ch)

    right, left = lax.rem(y + 1, ny), lax.rem(y + ny - 1, ny)
    steps = (ny // 2, ny - 1 - ny // 2)

    def hop(ch, m, way, s):
        own = lax.rem(y + ny - s, ny) if way == 0 else lax.rem(y + s, ny)
        part = zb.at[ch, m, pl.ds(own * up, up)]
        return remote(
            part, part, ags.at[0, ch, m, way, s], ags.at[1, ch, m, way, s],
            to_y(right if way == 0 else left),
        )

    def landed(ch, m, way, s):
        own = lax.rem(y + ny - s - 1, ny) if way == 0 else lax.rem(y + s + 1, ny)
        part = zb.at[ch, m, pl.ds(own * up, up)]
        return remote(
            part, part, ags.at[0, ch, m, way, s], ags.at[1, ch, m, way, s],
            to_y(left if way == 0 else right),
        )

    def pass_on(ch, s):
        for m in range(zbits):
            @pl.when(bit(z, m))
            def _():
                for way in range(2):
                    if s < steps[way]:
                        if s:
                            landed(ch, m, way, s - 1).wait_recv()
                        hop(ch, m, way, s).start()

    def before_y(lo):
        gap = jnp.zeros((groups, LANES), F32)
        for j in range(ny):
            gap = gap + jnp.where(jnp.logical_and(j >= lo, j < y), tau[j], 0.0)
        return gap

    def before_z(lo):
        gap = jnp.zeros((groups, LANES), F32)
        for j in range(nz):
            gap = gap + jnp.where(jnp.logical_and(j >= lo, j < z), lt[j], 0.0)
        return gap

    def put(ch, slot, part, gap):
        scale = jnp.exp(gap)
        for p in range(gc):
            for r in range(SPLIT):
                bks[ch, slot, r * rp:(r + 1) * rp, p * LANES:(p + 1) * LANES] = (
                    part[p * SPLIT + r].astype(F32) * scale[ch * gc + p:ch * gc + p + 1, :]
                ).astype(BF16)

    def put_y(ch):
        for m in range(ybits):
            @pl.when(bit(y, m))
            def _():
                if m == 0:
                    move_l0(ch, y - 1).wait_recv()
                else:
                    for j in y_round:
                        move_yb(ch, m, j, j).wait_recv()
                put(ch, m, yb.at[ch, m], before_y(lax.div(y, 1 << m) * (1 << m)))

            @pl.when(jnp.logical_not(bit(y, m)))
            def _():
                bks[ch, m] = jnp.zeros((STATE, wc), BF16)

    def put_z(ch):
        for m in range(zbits):
            @pl.when(bit(z, m))
            def _():
                for way in range(2):
                    if steps[way]:
                        landed(ch, m, way, steps[way] - 1).wait_recv()
                put(
                    ch, ybits + m, zb.at[ch, m],
                    before_y(0) + before_z(lax.div(z, 1 << m) * (1 << m)),
                )

            @pl.when(jnp.logical_not(bit(z, m)))
            def _():
                bks[ch, ybits + m] = jnp.zeros((STATE, wc), BF16)

    def cross(ch, t, cols, levels):
        full = slice(ch * wc + cols.start, ch * wc + cols.stop)
        cp = cpair(t)
        acc = None
        for m in levels:
            term = we[hbits + m, t, :, full].astype(F32) * dot(cp, bks[ch, m, :, cols])
            acc = term if acc is None else acc + term
        acc = scaled(
            acc, wide_rows(pg[2 * t], ch, cols), wide_rows(pg[2 * t + 1], ch, cols)
        )
        return acc + li[t, :, full]

    def cross_y(ch):
        def one(t, _):
            for cols in tiles:
                full = slice(ch * wc + cols.start, ch * wc + cols.stop)
                li[t, :, full] = cross(ch, t, cols, range(ybits))
            return 0

        lax.fori_loop(0, nh // 2, one, 0)

    def cross_z(ch, t):
        for cols in tiles:
            v = cross(ch, t, cols, range(ybits, ybits + zbits)).astype(BF16)
            io[ch, 2 * t, :, cols] = v[:SPAN]
            io[ch, 2 * t + 1, :, cols] = v[SPAN:]

    def return_rows():
        def one(p, _):
            cols = pl.ds(pl.multiple_of(p * LANES, LANES), LANES)
            er[:, cols] = spread(rows[1], 2 * p)
            return 0

        lax.fori_loop(0, HEADS // 2, one, 0, unroll=4)

    def z_sums(ch):
        for i in range(1, nz):
            @pl.when(z - i >= 0)
            def _():
                recv_r2(ch, i).wait_recv()
        for m in range(zbits):
            @pl.when(bit(z, m))
            def _():
                base = lax.div(z, 1 << m) * (1 << m)
                for q in range(up):
                    acc = r2[ch, base - 1, q].astype(F32)
                    gap = lt[base - 1, row_of(ch, q), :]
                    for i in range(2, (1 << m) + 1):
                        acc = acc + r2[ch, base - i, q].astype(F32) * jnp.exp(gap)
                        gap = gap + lt[base - i, row_of(ch, q), :]
                    zb[ch, m, y * up + q] = acc.astype(BF16)
        pass_on(ch, 0)

    def give_back(ch, i):
        if i < len(chips_round):
            cross_z(ch, chips_round[i])
            for j in heads_round[2 * i:2 * i + 2]:
                move_o(ch, j, hd).start()
        elif i == len(chips_round):
            cross_z(ch, chip)
            move_o(ch, heads_round[-1], hd).start()
            ir[ch, hd] = io[ch, hd]

    z_sums(0)
    line_sums(1)
    pass_on(0, 1)
    return_rows()
    pass_on(0, 2)
    put_y(0)
    cross_y(0)
    pass_on(0, 3)
    z_sums(1)
    put_y(1)
    cross_y(1)
    pass_on(1, 1)
    put_z(0)
    give_back(0, 0)
    give_back(0, 1)
    pass_on(1, 2)
    give_back(0, 2)
    give_back(0, 3)
    pass_on(1, 3)
    put_z(1)
    for i in range(4):
        give_back(1, i)

    def finish(ch, j):
        def one(p, _):
            at = j * groups + ch * gc + p
            cols = pl.ds(pl.multiple_of(at * LANES, LANES), LANES)
            part = pl.ds(pl.multiple_of(p * LANES, LANES), LANES)
            out[:, cols] = (
                o0[:, cols] + er[:, cols] * ir[ch, j, :, part].astype(F32)
            ).astype(BF16)
            return 0

        lax.fori_loop(0, gc, one, 0, unroll=4)

    for ch in chunks:
        finish(ch, hd)
        for j in heads_round[::-1]:
            move_o(ch, j, j).wait_recv()
            finish(ch, j)

    for j in heads_round:
        move_a(j, hd).wait_send()
        move_b(j, hd).wait_send()
        move_c(j, hd).wait_send()
        for ch in chunks:
            move_x(ch, j, hd).wait_send()
            move_o(ch, j, hd).wait_send()
    for j in y_round:
        move_tau(j, y).wait_send()
        for ch in chunks:
            move_r1(ch, j, y).wait_send()
        for m in range(1, ybits):
            @pl.when(bit(j, m))
            def _():
                for ch in chunks:
                    move_yb(ch, m, j, y).wait_send()

    @pl.when(lax.rem(y, 2) == 0)
    def _():
        for ch in chunks:
            move_l0(ch, y + 1).wait_send()

    for i in range(1, nz):
        @pl.when(z + i < nz)
        def _():
            send_lt(i).wait_send()
            for ch in chunks:
                send_r2(ch, i).wait_send()
    for s in range(steps[0]):
        for m in range(zbits):
            @pl.when(bit(z, m))
            def _():
                for ch in chunks:
                    for way in range(2):
                        if s < steps[way]:
                            hop(ch, m, way, s).wait_send()


def on_device(nh, ny, nz, token_inputs, state_in, state_out, log_decay, token_codes, table, gain):
    hl = HEADS // nh
    groups = hl // 2
    gc = groups // CHUNKS
    units = gc * SPLIT
    up = units // ny
    rp = STATE // SPLIT
    wide = hl * HEAD_DIM
    wc = wide // CHUNKS
    hbits, ybits, zbits = bits_of(nh), bits_of(ny), bits_of(nz)
    nlev = hbits + ybits + zbits
    vm = pltpu.VMEM
    sem = pltpu.SemaphoreType.DMA
    pieces = max(sum(ny >> (m + 1) for m in range(1, ybits)), 1)
    nc = CHUNKS
    zb = max(zbits, 1)
    return pl.pallas_call(
        functools.partial(kernel, nh, ny, nz),
        out_shape=jax.ShapeDtypeStruct((SPAN, HEADS * HEAD_DIM), BF16),
        in_specs=[pl.BlockSpec(memory_space=pltpu.HBM)] * 7,
        out_specs=pl.BlockSpec(memory_space=pltpu.VMEM),
        scratch_shapes=[
            vm((SPAN, HEADS * HEAD_DIM), BF16),
            vm((SPAN, HEADS), BF16),
            vm((1, SPAN), jnp.int32),
            vm((CODES, LEVELS * HEADS), BF16),
            vm((1, HEADS), F32),
            vm((nc, nh, SPAN, wc), BF16),
            vm((nc, nh, SPAN, wc), BF16),
            vm((nh, SPAN, STATE), BF16),
            vm((nh, SPAN, STATE), BF16),
            vm((nh, groups + 8, LANES), F32),
            vm((nh, groups + 8, LANES), F32),
            vm((SPAN, HEADS * HEAD_DIM), F32),
            vm((SPAN, HEADS * HEAD_DIM), F32),
            vm((2, SPAN, LANES), F32),
            vm((nlev, CODES, wide), BF16),
            vm((nh * SPAN, CODES), BF16),
            vm((nlev, nh // 2, 2 * SPAN, wide), BF16),
            vm((nh, STATE, wc), F32),
            vm((nc, nh - 1, STATE, wc), BF16),
            vm((nh // 2, 2 * SPAN, wide), F32),
            vm((nc, units, rp, LANES), BF16),
            vm((nc, ny, up, rp, LANES), BF16),
            vm((nc, pieces, up, rp, LANES), BF16),
            vm((nc, up, rp, LANES), BF16),
            vm((nc, nz, up, rp, LANES), BF16),
            vm((nc, ybits, units, rp, LANES), BF16),
            vm((nc, zb, units, rp, LANES), BF16),
            vm((nc, ybits + zbits, STATE, wc), BF16),
            vm((ny, groups, LANES), F32),
            vm((nz, groups, LANES), F32),
            vm((nh, groups, LANES), F32),
            vm((nc, nh, SPAN, wc), BF16),
            vm((nc, nh, SPAN, wc), BF16),
            sem((7,)),
            sem((2, nc, nh)),
            sem((2, nh)),
            sem((2, nh)),
            sem((2, nh)),
            sem((2, ny)),
            sem((2, nz)),
            sem((2, nc, ny)),
            sem((2, nc)),
            sem((2, nc, max(ybits, 1), ny)),
            sem((2, nc, nz)),
            sem((2, nc, zb, 2, max(ny // 2, 1))),
            sem((2, nc, nh)),
        ],
        compiler_params=pltpu.CompilerParams(
            collective_id=0, has_side_effects=True, vmem_limit_bytes=VMEM_LIMIT
        ),
    )(*(
        pltpu.with_memory_space_constraint(v, pltpu.HBM)
        for v in (
            token_inputs, state_in, state_out, log_decay,
            token_codes.reshape(1, SPAN), table, gain.reshape(1, HEADS),
        )
    ))


def solution(mesh, ny=NY):
    nh = mesh.shape["head"]
    nz = mesh.shape["ctx"] // ny
    return jax.shard_map(
        functools.partial(on_device, nh, ny, nz),
        mesh=mesh,
        in_specs=(
            P(("ctx", "head"), None),
            P(("ctx", "head"), None),
            P(("ctx", "head"), None),
            P(("ctx", "head"), None),
            P(("ctx", "head")),
            P(),
            P(),
        ),
        out_specs=P(("ctx", "head"), None),
        check_vma=False,
    )
```

```python
import functools

import jax
import jax.numpy as jnp
from jax import lax
from jax.experimental import pallas as pl
from jax.experimental.pallas import tpu as pltpu
from jax.sharding import PartitionSpec as P

HEADS = 128
HEAD_DIM = 64
STATE = 128
SPAN = 64
LEVELS = 11
CODES = 64
NY = 8
LANES = 128
CHUNKS = 2
SPLIT = 2
TILE = 256
VMEM_LIMIT = 44 << 20
MESH = pl.DeviceIdType.MESH
F32 = jnp.float32
BF16 = jnp.bfloat16


def bits_of(n):
    return n.bit_length() - 1


def dot(a, b):
    return jnp.dot(a, b, preferred_element_type=F32)


def dot_t(a, b):
    return lax.dot_general(a, b, (((0,), (0,)), ((), ())), preferred_element_type=F32)


def iota(shape, dim):
    return lax.broadcasted_iota(jnp.int32, shape, dim)


def spread(v, first):
    idx = first + (iota(v.shape, 1) >> 6)
    return jnp.take_along_axis(v, idx, axis=1, mode="promise_in_bounds")


def kernel(
    nh, ny, nz,
    x_in, b_in, c_in, d_in, codes_in, tab_in, skip_in, out,
    x, d, codes, tab, skip,
    xc, xr, br, cr, aux, auxr, o0, er, rows, te, oh, we, sg, lbs, li,
    sb, r1, pb, tz, r2, yb, zb, bks, tau, lt, pg, io, ir, rl,
    ins, xs, bs, cs, axs, taus, lts, r1s, l0s, ys, r2s, ags, ios, rls, fws,
):
    hl = HEADS // nh
    groups = hl // 2
    gc = groups // CHUNKS
    units = gc * SPLIT
    up = units // ny
    rp = STATE // SPLIT
    wc = gc * LANES
    tiles = [slice(i, i + TILE) for i in range(0, wc, TILE)]
    hbits, ybits, zbits = bits_of(nh), bits_of(ny), bits_of(nz)
    nlev = hbits + ybits + zbits
    chunks = range(CHUNKS)
    hd = lax.axis_index("head")
    k = lax.axis_index("ctx")
    y = lax.rem(k, ny)
    z = lax.div(k, ny)
    chip, core = lax.div(hd, 2), lax.rem(hd, 2)

    def to_head(j):
        return {"head": j}

    def to_y(j):
        return {"ctx": z * ny + j}

    def to_z(j):
        return {"ctx": j * ny + y}

    def remote(src, dst, send, recv, where):
        return pltpu.make_async_remote_copy(
            src_ref=src, dst_ref=dst, send_sem=send, recv_sem=recv,
            device_id=where, device_id_type=MESH,
        )

    def bit(v, m):
        return lax.rem(lax.div(v, 1 << m), 2) == 1

    hops = sorted(range(1, nh // 2), key=lambda o: -min(o, nh // 2 - o))
    chips_round = [lax.rem(chip + o, nh // 2) for o in hops]
    heads_round = []
    for q in chips_round:
        heads_round += [2 * q + core, 2 * q + 1 - core]
    heads_round.append(2 * chip + 1 - core)
    relayed = nh == 8
    near_heads = heads_round[2:] if relayed else heads_round
    far = lax.rem(chip + 2, nh // 2)
    mid = lax.rem(chip + 1 + 2 * core, nh // 2)
    helped = 2 * lax.rem(chip + 3 - 2 * core, nh // 2) + core
    y_round = [lax.rem(y + i, ny) for i in range(1, ny)]
    z_round = [lax.rem(z + i, nz) for i in range(1, nz)]

    lt[...] = jnp.zeros_like(lt)
    barrier = pltpu.get_barrier_semaphore()
    for j in heads_round:
        pl.semaphore_signal(barrier, inc=1, device_id=to_head(j), device_id_type=MESH)
    for j in y_round:
        pl.semaphore_signal(barrier, inc=1, device_id=to_y(j), device_id_type=MESH)
    for j in z_round:
        pl.semaphore_signal(barrier, inc=1, device_id=to_z(j), device_id_type=MESH)

    loads = [
        pltpu.make_async_copy(src, dst, ins.at[i])
        for i, (src, dst) in enumerate((
            (d_in, d), (x_in, x), (b_in, br.at[hd]), (c_in, cr.at[hd]),
            (codes_in, codes), (tab_in, tab), (skip_in, skip),
        ))
    ]
    for load in loads:
        load.start()
    b, c = br.at[hd], cr.at[hd]

    loads[0].wait()
    lower = iota((SPAN, SPAN), 0) >= iota((SPAN, SPAN), 1)
    run = dot(jnp.where(lower, 1.0, 0.0).astype(BF16), d[...])
    tot = run[SPAN - 1:SPAN, :]
    fac = jnp.exp(tot - run)

    def carry(ch, j):
        def one(p, _):
            cols = pl.ds(pl.multiple_of(p * LANES, LANES), LANES)
            at = j * groups + ch * gc + p
            src = pl.ds(pl.multiple_of(at * LANES, LANES), LANES)
            m = spread(fac, 2 * at)
            xc[ch, j, :, cols] = (m * x[:, src].astype(F32)).astype(BF16)
            return 0

        lax.fori_loop(0, gc, one, 0, unroll=4)

    def move_x(ch, j, src):
        return remote(
            xc.at[ch, j], xr.at[ch, src], xs.at[0, ch, j], xs.at[1, ch, src], to_head(j)
        )

    def move_b(j, src):
        return remote(b, br.at[src], bs.at[0, j], bs.at[1, src], to_head(j))

    def move_c(j, src):
        return remote(c, cr.at[src], cs.at[0, j], cs.at[1, src], to_head(j))

    def move_a(j, src):
        return remote(aux.at[j], auxr.at[src], axs.at[0, j], axs.at[1, src], to_head(j))

    def move_o(ch, j, src):
        return remote(
            io.at[ch, j], ir.at[ch, src], ios.at[0, ch, j], ios.at[1, ch, src], to_head(j)
        )

    def share_aux():
        pairs = HEADS // 2
        first = 2 * iota((pairs, LANES), 0) + (iota((pairs, LANES), 1) >> 6)
        tot_pairs = jnp.take_along_axis(
            jnp.broadcast_to(tot, (pairs, LANES)), first, axis=1, mode="promise_in_bounds"
        )
        code_row = codes[...].astype(F32)
        for j in range(nh):
            aux[j, 0:groups, :] = tot_pairs[j * groups:(j + 1) * groups, :]
            aux[j, groups:groups + 8, 0:SPAN] = jnp.broadcast_to(code_row, (8, SPAN))
            aux[j, groups:groups + 8, SPAN:] = jnp.zeros((8, LANES - SPAN), F32)
        auxr[hd] = aux[hd]
        for j in heads_round:
            move_a(j, hd).start()

    def relay(kind, ch):
        src = (xc, io)[kind].at[ch, pl.ds(2 * far, 2)]
        return remote(
            src, rl.at[kind, ch], rls.at[0, kind, ch], rls.at[1, kind, ch], to_head(2 * mid + core)
        )

    def forward(kind, ch, f):
        dst, sems = ((xr, xs), (ir, ios))[kind]
        return remote(
            rl.at[kind, ch, f], dst.at[ch, helped], fws.at[kind, ch, f],
            sems.at[1, ch, helped], to_head(2 * mid + f),
        )

    def hand_on(kind, ch):
        if relayed:
            relay(kind, ch).wait_recv()
            for f in range(2):
                forward(kind, ch, f).start()

    def send_far(ch):
        if relayed:
            for j in heads_round[:2]:
                carry(ch, j)
            relay(0, ch).start()

    for load in loads[1:]:
        load.wait()
    carry(0, heads_round[0])
    pl.semaphore_wait(barrier, (nh - 1) + (ny - 1) + (nz - 1))
    if relayed:
        carry(0, heads_round[1])
        relay(0, 0).start()
    for i, j in enumerate(near_heads):
        if i or relayed:
            carry(0, j)
        move_x(0, j, hd).start()
        move_b(j, hd).start()
    for j in heads_round[:len(heads_round) - len(near_heads)]:
        move_b(j, hd).start()
    send_far(1)
    share_aux()
    cols0 = iota((LEVELS * HEADS, LANES), 0)
    lane0 = iota((LEVELS * HEADS, LANES), 1)
    tab0 = dot(tab[...], jnp.where(cols0 == lane0 * LEVELS, 1.0, 0.0).astype(BF16)).astype(BF16)
    code_row = codes[...].astype(F32)
    code_t = jnp.where(
        jnp.broadcast_to(code_row, (CODES, SPAN)) == iota((CODES, SPAN), 0).astype(F32), 1.0, 0.0
    ).astype(BF16)
    w0 = dot_t(code_t, tab0)
    rows[0] = w0 * jnp.exp(run - tot)
    rows[1] = jnp.exp(run)

    per = LANES // hl
    for t in range(-(-nlev // per)):
        lev = 1 + t * per + lane0 // hl
        want = (hd * hl + lax.rem(lane0, hl)) * LEVELS + lev
        picked = dot(tab[...], jnp.where(cols0 == want, 1.0, 0.0).astype(BF16))
        for l in range(t * per, min(nlev, (t + 1) * per)):
            for p in range(groups):
                te[l, :, p * LANES:(p + 1) * LANES] = spread(
                    picked, (l - t * per) * hl + 2 * p
                ).astype(BF16)
    hand_on(0, 0)
    for j in near_heads:
        carry(1, j)
        move_x(1, j, hd).start()
    for ch in chunks:
        carry(ch, hd)
        xr[ch, hd] = xc[ch, hd]

    for j in heads_round:
        move_a(j, j).wait_recv()
    mine = auxr[0, 0:groups, :]
    for g in range(nh):
        pg[g] = jnp.exp(mine) if g else jnp.ones((groups, LANES), F32)
        if g:
            mine = mine + auxr[g, 0:groups, :]
    tau[y] = mine

    def move_tau(j, src):
        return remote(tau.at[y], tau.at[src], taus.at[0, j], taus.at[1, src], to_y(j))

    for j in y_round:
        move_tau(j, y).start()

    eye = jnp.where(iota((CODES, CODES), 0) == iota((CODES, CODES), 1), 1.0, 0.0).astype(BF16)
    for g in range(nh):
        row = auxr[g, groups:groups + 1, 0:SPAN]
        hot = jnp.where(
            jnp.broadcast_to(row, (CODES, SPAN)) == iota((CODES, SPAN), 0).astype(F32), 1.0, 0.0
        ).astype(BF16)
        oh[g * SPAN:(g + 1) * SPAN, :] = dot_t(hot, eye).astype(BF16)

    def weigh(l, cols, g0, g1):
        w = dot(oh[g0 * SPAN:g1 * SPAN, :], te[l, :, cols]).astype(BF16)
        for t in range(g0 // 2, g1 // 2):
            we[l, t, :, cols] = w[(2 * t - g0) * SPAN:(2 * t + 2 - g0) * SPAN]

    for l in range(nlev):
        for i in range(0, groups * LANES, TILE):
            if l < hbits and l > 0:
                for g in range(2 << l >> 1, nh, 2 << l):
                    weigh(l, slice(i, i + TILE), g, g + (1 << l))
            else:
                weigh(l, slice(i, i + TILE), 0, nh)

    hand_on(0, 1)
    for j in heads_round:
        move_c(j, hd).start()

    scores = lax.dot_general(
        c[...], b[...], (((1,), (1,)), ((), ())), preferred_element_type=F32
    )
    near = jnp.where(lower, scores, 0.0).astype(BF16)
    gain = jnp.broadcast_to(skip[...], (SPAN, LANES))

    def level0(j, _):
        for ch in chunks:
            v = dot(near, xc[ch, j])
            for p in range(gc):
                at = j * groups + ch * gc + p
                cols = pl.ds(pl.multiple_of(at * LANES, LANES), LANES)
                o0[:, cols] = (
                    spread(rows[0], 2 * at) * v[:, p * LANES:(p + 1) * LANES]
                    + spread(gain, 2 * at) * x[:, cols].astype(F32)
                )
        return 0

    lax.fori_loop(0, nh, level0, 0)

    for j in y_round:
        move_tau(j, j).wait_recv()
    line = tau[0]
    for j in range(1, ny):
        line = line + tau[j]
    lt[z] = line

    def send_lt(i):
        return remote(lt.at[z], lt.at[z], lts.at[0, z + i], lts.at[1, z], to_z(z + i))

    def recv_lt(i):
        return remote(lt.at[z], lt.at[z - i], lts.at[0, z], lts.at[1, z - i], to_z(z - i))

    for i in range(1, nz):
        @pl.when(z + i < nz)
        def _():
            send_lt(i).start()

    offs = [0]
    for m in range(hbits):
        offs.append(offs[-1] + (nh >> (m + 1)))

    def fold(ch):
        def one(p, _):
            cols = pl.ds(pl.multiple_of(p * LANES, LANES), LANES)
            cur = [sg[g, :, cols] for g in range(nh)]
            dec = [auxr[g, pl.ds(ch * gc + p, 1), :] for g in range(nh)]
            for m in range(hbits):
                new, new_dec = [], []
                for i in range(len(cur) // 2):
                    lbs[ch, offs[m] + i, :, cols] = cur[2 * i].astype(BF16)
                    new.append(cur[2 * i] * jnp.exp(dec[2 * i + 1]) + cur[2 * i + 1])
                    new_dec.append(dec[2 * i] + dec[2 * i + 1])
                cur, dec = new, new_dec
            for r in range(SPLIT):
                sb[ch, p * SPLIT + r] = cur[0][r * rp:(r + 1) * rp].astype(BF16)
            return 0

        lax.fori_loop(0, gc, one, 0)

    def move_r1(ch, j, src):
        return remote(
            sb.at[ch, pl.ds(j * up, up)], r1.at[ch, src],
            r1s.at[0, ch, j], r1s.at[1, ch, src], to_y(j),
        )

    def move_l0(ch, j):
        return remote(sb.at[ch], yb.at[ch, 0], l0s.at[0, ch], l0s.at[1, ch], to_y(j))

    for ch in chunks:
        sg[hd] = dot_t(br[hd], xr[ch, hd])
        for j in reversed(heads_round):
            if ch == 0:
                move_b(j, j).wait_recv()
            move_x(ch, j, j).wait_recv()
            sg[j] = dot_t(br[j], xr[ch, j])
        fold(ch)
        for j in y_round:
            move_r1(ch, j, y).start()

        @pl.when(lax.rem(y, 2) == 0)
        def _():
            move_l0(ch, y + 1).start()

        for q in range(up):
            r1[ch, y, q] = sb[ch, y * up + q]

    for i in range(1, nz):
        @pl.when(z - i >= 0)
        def _():
            recv_lt(i).wait_recv()

    yoffs = [0]
    for m in range(1, ybits):
        yoffs.append(yoffs[-1] + (ny >> (m + 1)))

    def row_of(ch, q):
        return pl.ds(ch * gc + lax.div(y * up + q, SPLIT), 1)

    def send_r2(ch, i):
        return remote(
            tz.at[ch], r2.at[ch, z], r2s.at[0, ch, z + i], r2s.at[1, ch, z], to_z(z + i)
        )

    def recv_r2(ch, i):
        return remote(
            tz.at[ch], r2.at[ch, z - i], r2s.at[0, ch, z], r2s.at[1, ch, z - i], to_z(z - i)
        )

    def move_yb(ch, m, j, src):
        return remote(
            pb.at[ch, yoffs[m - 1] + lax.div(j, 2 << m)], yb.at[ch, m, pl.ds(src * up, up)],
            ys.at[0, ch, m, j], ys.at[1, ch, m, src], to_y(j),
        )

    def line_sums(ch):
        for j in y_round:
            move_r1(ch, j, j).wait_recv()
        for q in range(up):
            cur = [r1[ch, j, q].astype(F32) for j in range(ny)]
            dec = [tau[j, row_of(ch, q), :] for j in range(ny)]
            for m in range(ybits):
                new, new_dec = [], []
                for i in range(len(cur) // 2):
                    if m:
                        pb[ch, yoffs[m - 1] + i, q] = cur[2 * i].astype(BF16)
                    new.append(cur[2 * i] * jnp.exp(dec[2 * i + 1]) + cur[2 * i + 1])
                    new_dec.append(dec[2 * i] + dec[2 * i + 1])
                cur, dec = new, new_dec
            r2[ch, z, q] = cur[0].astype(BF16)
            tz[ch, q] = cur[0].astype(BF16)
        for i in range(1, nz):
            @pl.when(z + i < nz)
            def _():
                send_r2(ch, i).start()
        for m in range(1, ybits):
            for j in y_round:
                @pl.when(bit(j, m))
                def _():
                    move_yb(ch, m, j, y).start()

            @pl.when(bit(y, m))
            def _():
                for q in range(up):
                    yb[ch, m, y * up + q] = pb[ch, yoffs[m - 1] + lax.div(y, 2 << m), q]

    line_sums(0)

    for j in heads_round:
        move_c(j, j).wait_recv()

    def cpair(t):
        return cr[pl.ds(2 * t, 2)].reshape(2 * SPAN, STATE)

    def scaled(v, row0, row1):
        return jnp.concatenate([v[:SPAN] * row0, v[SPAN:] * row1], axis=0)

    def gap_rows(lo, g):
        gap = jnp.zeros((groups, LANES), F32)
        for before in range(lo, g):
            gap = gap + auxr[before, 0:groups, :]
        return jnp.exp(gap)

    def wide_rows(tile, ch, cols):
        at = [ch * gc + i // LANES for i in range(cols.start, cols.stop, LANES)]
        return jnp.concatenate([tile[i:i + 1, :] for i in at], axis=1)

    def inner(ch):
        for t in range(nh // 2):
            cp = cpair(t)
            for cols in tiles:
                full = slice(ch * wc + cols.start, ch * wc + cols.stop)
                v = dot(cp[SPAN:], lbs[ch, t, :, cols]) * we[0, t, SPAN:, full].astype(F32)
                acc = None
                for m in range(1, hbits):
                    if not 2 * t >> m & 1:
                        continue
                    lo = 2 * t >> m << m
                    term = we[m, t, :, full].astype(F32) * dot(
                        cp, lbs[ch, offs[m] + (2 * t >> (m + 1)), :, cols]
                    )
                    term = scaled(
                        term,
                        wide_rows(gap_rows(lo, 2 * t), ch, cols),
                        wide_rows(gap_rows(lo, 2 * t + 1), ch, cols),
                    )
                    acc = term if acc is None else acc + term
                if acc is None:
                    li[t, :SPAN, full] = jnp.zeros((SPAN, TILE), F32)
                    li[t, SPAN:, full] = v
                else:
                    li[t, :SPAN, full] = acc[:SPAN]
                    li[t, SPAN:, full] = acc[SPAN:] + v

    for ch in chunks:
        inner(ch)

    right, left = lax.rem(y + 1, ny), lax.rem(y + ny - 1, ny)
    steps = (ny - 1 - ny // 2, ny // 2)

    def hop(ch, m, way, s):
        own = lax.rem(y + ny - s, ny) if way == 0 else lax.rem(y + s, ny)
        part = zb.at[ch, m, pl.ds(own * up, up)]
        return remote(
            part, part, ags.at[0, ch, m, way, s], ags.at[1, ch, m, way, s],
            to_y(right if way == 0 else left),
        )

    def landed(ch, m, way, s):
        own = lax.rem(y + ny - s - 1, ny) if way == 0 else lax.rem(y + s + 1, ny)
        part = zb.at[ch, m, pl.ds(own * up, up)]
        return remote(
            part, part, ags.at[0, ch, m, way, s], ags.at[1, ch, m, way, s],
            to_y(left if way == 0 else right),
        )

    def pass_on(ch, s):
        for m in range(zbits):
            @pl.when(bit(z, m))
            def _():
                for way in range(2):
                    if s < steps[way]:
                        if s:
                            landed(ch, m, way, s - 1).wait_recv()
                        hop(ch, m, way, s).start()

    def before_y(lo):
        gap = jnp.zeros((groups, LANES), F32)
        for j in range(ny):
            gap = gap + jnp.where(jnp.logical_and(j >= lo, j < y), tau[j], 0.0)
        return gap

    def before_z(lo):
        gap = jnp.zeros((groups, LANES), F32)
        for j in range(nz):
            gap = gap + jnp.where(jnp.logical_and(j >= lo, j < z), lt[j], 0.0)
        return gap

    def put(ch, slot, part, gap):
        scale = jnp.exp(gap)
        for p in range(gc):
            for r in range(SPLIT):
                bks[ch, slot, r * rp:(r + 1) * rp, p * LANES:(p + 1) * LANES] = (
                    part[p * SPLIT + r].astype(F32) * scale[ch * gc + p:ch * gc + p + 1, :]
                ).astype(BF16)

    def put_y(ch):
        for m in range(ybits):
            @pl.when(bit(y, m))
            def _():
                if m == 0:
                    move_l0(ch, y - 1).wait_recv()
                else:
                    for j in y_round:
                        move_yb(ch, m, j, j).wait_recv()
                put(ch, m, yb.at[ch, m], before_y(lax.div(y, 1 << m) * (1 << m)))

            @pl.when(jnp.logical_not(bit(y, m)))
            def _():
                bks[ch, m] = jnp.zeros((STATE, wc), BF16)

    def put_z(ch):
        for m in range(zbits):
            @pl.when(bit(z, m))
            def _():
                for way in range(2):
                    if steps[way]:
                        landed(ch, m, way, steps[way] - 1).wait_recv()
                put(
                    ch, ybits + m, zb.at[ch, m],
                    before_y(0) + before_z(lax.div(z, 1 << m) * (1 << m)),
                )

            @pl.when(jnp.logical_not(bit(z, m)))
            def _():
                bks[ch, ybits + m] = jnp.zeros((STATE, wc), BF16)

    def cross(ch, t, cols, levels):
        full = slice(ch * wc + cols.start, ch * wc + cols.stop)
        cp = cpair(t)
        if not levels:
            return li[t, :, full]
        acc = None
        for m in levels:
            term = we[hbits + m, t, :, full].astype(F32) * dot(cp, bks[ch, m, :, cols])
            acc = term if acc is None else acc + term
        acc = scaled(
            acc, wide_rows(pg[2 * t], ch, cols), wide_rows(pg[2 * t + 1], ch, cols)
        )
        return acc + li[t, :, full]

    def cross_y(ch):
        def one(t, _):
            for cols in tiles:
                full = slice(ch * wc + cols.start, ch * wc + cols.stop)
                li[t, :, full] = cross(ch, t, cols, range(ybits))
            return 0

        lax.fori_loop(0, nh // 2, one, 0)

    def cross_z(ch, t):
        for cols in tiles:
            v = cross(ch, t, cols, range(ybits, ybits + zbits)).astype(BF16)
            io[ch, 2 * t, :, cols] = v[:SPAN]
            io[ch, 2 * t + 1, :, cols] = v[SPAN:]

    def return_rows():
        def one(p, _):
            cols = pl.ds(pl.multiple_of(p * LANES, LANES), LANES)
            er[:, cols] = spread(rows[1], 2 * p)
            return 0

        lax.fori_loop(0, HEADS // 2, one, 0, unroll=4)

    def z_sums(ch):
        for i in range(1, nz):
            @pl.when(z - i >= 0)
            def _():
                recv_r2(ch, i).wait_recv()
        for m in range(zbits):
            @pl.when(bit(z, m))
            def _():
                base = lax.div(z, 1 << m) * (1 << m)
                for q in range(up):
                    acc = r2[ch, base - 1, q].astype(F32)
                    gap = lt[base - 1, row_of(ch, q), :]
                    for i in range(2, (1 << m) + 1):
                        acc = acc + r2[ch, base - i, q].astype(F32) * jnp.exp(gap)
                        gap = gap + lt[base - i, row_of(ch, q), :]
                    zb[ch, m, y * up + q] = acc.astype(BF16)
        pass_on(ch, 0)

    def give_back(ch, i):
        if i < len(chips_round):
            cross_z(ch, chips_round[i])
            if relayed and i == 0:
                relay(1, ch).start()
            else:
                for j in heads_round[2 * i:2 * i + 2]:
                    move_o(ch, j, hd).start()
        elif i == len(chips_round):
            cross_z(ch, chip)
            move_o(ch, heads_round[-1], hd).start()
            ir[ch, hd] = io[ch, hd]

    z_sums(0)
    line_sums(1)
    pass_on(0, 1)
    return_rows()
    pass_on(0, 2)
    put_y(0)
    cross_y(0)
    pass_on(0, 3)
    z_sums(1)
    put_y(1)
    cross_y(1)
    pass_on(1, 1)
    put_z(0)
    give_back(0, 0)
    give_back(0, 1)
    pass_on(1, 2)
    give_back(0, 2)
    give_back(0, 3)
    pass_on(1, 3)
    hand_on(1, 0)
    put_z(1)
    for i in range(4):
        give_back(1, i)

    def finish(ch, j):
        def one(p, _):
            at = j * groups + ch * gc + p
            cols = pl.ds(pl.multiple_of(at * LANES, LANES), LANES)
            part = pl.ds(pl.multiple_of(p * LANES, LANES), LANES)
            out[:, cols] = (
                o0[:, cols] + er[:, cols] * ir[ch, j, :, part].astype(F32)
            ).astype(BF16)
            return 0

        lax.fori_loop(0, gc, one, 0, unroll=4)

    for ch in chunks:
        if ch:
            hand_on(1, ch)
        finish(ch, hd)
        for j in heads_round[::-1]:
            move_o(ch, j, j).wait_recv()
            finish(ch, j)

    for j in heads_round:
        move_a(j, hd).wait_send()
        move_b(j, hd).wait_send()
        move_c(j, hd).wait_send()
    for ch in chunks:
        for j in near_heads:
            move_x(ch, j, hd).wait_send()
            move_o(ch, j, hd).wait_send()
        if relayed:
            for kind in range(2):
                relay(kind, ch).wait_send()
                for f in range(2):
                    forward(kind, ch, f).wait_send()
    for j in y_round:
        move_tau(j, y).wait_send()
        for ch in chunks:
            move_r1(ch, j, y).wait_send()
        for m in range(1, ybits):
            @pl.when(bit(j, m))
            def _():
                for ch in chunks:
                    move_yb(ch, m, j, y).wait_send()

    @pl.when(lax.rem(y, 2) == 0)
    def _():
        for ch in chunks:
            move_l0(ch, y + 1).wait_send()

    for i in range(1, nz):
        @pl.when(z + i < nz)
        def _():
            send_lt(i).wait_send()
            for ch in chunks:
                send_r2(ch, i).wait_send()
    for s in range(max(steps)):
        for m in range(zbits):
            @pl.when(bit(z, m))
            def _():
                for ch in chunks:
                    for way in range(2):
                        if s < steps[way]:
                            hop(ch, m, way, s).wait_send()


def on_device(nh, ny, nz, token_inputs, state_in, state_out, log_decay, token_codes, table, gain):
    hl = HEADS // nh
    groups = hl // 2
    gc = groups // CHUNKS
    units = gc * SPLIT
    up = units // ny
    rp = STATE // SPLIT
    wide = hl * HEAD_DIM
    wc = wide // CHUNKS
    hbits, ybits, zbits = bits_of(nh), bits_of(ny), bits_of(nz)
    nlev = hbits + ybits + zbits
    vm = pltpu.VMEM
    sem = pltpu.SemaphoreType.DMA
    pieces = max(sum(ny >> (m + 1) for m in range(1, ybits)), 1)
    nc = CHUNKS
    zb = max(zbits, 1)
    return pl.pallas_call(
        functools.partial(kernel, nh, ny, nz),
        out_shape=jax.ShapeDtypeStruct((SPAN, HEADS * HEAD_DIM), BF16),
        in_specs=[pl.BlockSpec(memory_space=pltpu.HBM)] * 7,
        out_specs=pl.BlockSpec(memory_space=pltpu.VMEM),
        scratch_shapes=[
            vm((SPAN, HEADS * HEAD_DIM), BF16),
            vm((SPAN, HEADS), BF16),
            vm((1, SPAN), jnp.int32),
            vm((CODES, LEVELS * HEADS), BF16),
            vm((1, HEADS), F32),
            vm((nc, nh, SPAN, wc), BF16),
            vm((nc, nh, SPAN, wc), BF16),
            vm((nh, SPAN, STATE), BF16),
            vm((nh, SPAN, STATE), BF16),
            vm((nh, groups + 8, LANES), F32),
            vm((nh, groups + 8, LANES), F32),
            vm((SPAN, HEADS * HEAD_DIM), F32),
            vm((SPAN, HEADS * HEAD_DIM), F32),
            vm((2, SPAN, LANES), F32),
            vm((nlev, CODES, wide), BF16),
            vm((nh * SPAN, CODES), BF16),
            vm((nlev, nh // 2, 2 * SPAN, wide), BF16),
            vm((nh, STATE, wc), F32),
            vm((nc, nh - 1, STATE, wc), BF16),
            vm((nh // 2, 2 * SPAN, wide), F32),
            vm((nc, units, rp, LANES), BF16),
            vm((nc, ny, up, rp, LANES), BF16),
            vm((nc, pieces, up, rp, LANES), BF16),
            vm((nc, up, rp, LANES), BF16),
            vm((nc, nz, up, rp, LANES), BF16),
            vm((nc, ybits, units, rp, LANES), BF16),
            vm((nc, zb, units, rp, LANES), BF16),
            vm((nc, ybits + zbits, STATE, wc), BF16),
            vm((ny, groups, LANES), F32),
            vm((nz, groups, LANES), F32),
            vm((nh, groups, LANES), F32),
            vm((nc, nh, SPAN, wc), BF16),
            vm((nc, nh, SPAN, wc), BF16),
            vm((2, nc, 2, SPAN, wc), BF16),
            sem((7,)),
            sem((2, nc, nh)),
            sem((2, nh)),
            sem((2, nh)),
            sem((2, nh)),
            sem((2, ny)),
            sem((2, nz)),
            sem((2, nc, ny)),
            sem((2, nc)),
            sem((2, nc, max(ybits, 1), ny)),
            sem((2, nc, nz)),
            sem((2, nc, zb, 2, max(ny // 2, 1))),
            sem((2, nc, nh)),
            sem((2, 2, nc)),
            sem((2, nc, 2)),
        ],
        compiler_params=pltpu.CompilerParams(
            collective_id=0, has_side_effects=True, vmem_limit_bytes=VMEM_LIMIT
        ),
    )(*(
        pltpu.with_memory_space_constraint(v, pltpu.HBM)
        for v in (
            token_inputs, state_in, state_out, log_decay,
            token_codes.reshape(1, SPAN), table, gain.reshape(1, HEADS),
        )
    ))


def solution(mesh, ny=NY):
    nh = mesh.shape["head"]
    nz = mesh.shape["ctx"] // ny
    return jax.shard_map(
        functools.partial(on_device, nh, ny, nz),
        mesh=mesh,
        in_specs=(
            P(("ctx", "head"), None),
            P(("ctx", "head"), None),
            P(("ctx", "head"), None),
            P(("ctx", "head"), None),
            P(("ctx", "head")),
            P(),
            P(),
        ),
        out_specs=P(("ctx", "head"), None),
        check_vma=False,
    )
```

```python
import functools

import jax
import jax.numpy as jnp
from jax import lax
from jax.experimental import pallas as pl
from jax.experimental.pallas import tpu as pltpu
from jax.sharding import PartitionSpec as P

HEADS = 128
HEAD_DIM = 64
STATE = 128
SPAN = 64
LEVELS = 11
CODES = 64
NY = 8
LANES = 128
CHUNKS = 2
SPLIT = 2
TILE = 256
VMEM_LIMIT = 44 << 20
MESH = pl.DeviceIdType.MESH
F32 = jnp.float32
BF16 = jnp.bfloat16


def bits_of(n):
    return n.bit_length() - 1


def far_first(n):
    return sorted(range(1, n), key=lambda i: -min(i, n - i))


def dot(a, b):
    return jnp.dot(a, b, preferred_element_type=F32)


def dot_t(a, b):
    return lax.dot_general(a, b, (((0,), (0,)), ((), ())), preferred_element_type=F32)


def iota(shape, dim):
    return lax.broadcasted_iota(jnp.int32, shape, dim)


def spread(v, first):
    idx = first + (iota(v.shape, 1) >> 6)
    return jnp.take_along_axis(v, idx, axis=1, mode="promise_in_bounds")


def kernel(
    nh, ny, nz,
    x_in, b_in, c_in, d_in, codes_in, tab_in, skip_in, out,
    x, d, codes, tab, skip,
    xc, xr, br, cr, aux, auxr, o0, er, rows, te, oh, we, sg, lbs, li,
    sb, r1, pb, tz, r2, yb, zb, bks, tau, lt, pg, io, ir,
    ins, xs, bs, cs, axs, taus, lts, r1s, l0s, ys, r2s, ags, ios,
):
    hl = HEADS // nh
    groups = hl // 2
    gc = groups // CHUNKS
    units = gc * SPLIT
    up = units // ny
    rp = STATE // SPLIT
    wc = gc * LANES
    tiles = [slice(i, i + TILE) for i in range(0, wc, TILE)]
    hbits, ybits, zbits = bits_of(nh), bits_of(ny), bits_of(nz)
    nlev = hbits + ybits + zbits
    chunks = range(CHUNKS)
    hd = lax.axis_index("head")
    k = lax.axis_index("ctx")
    y = lax.rem(k, ny)
    z = lax.div(k, ny)
    chip, core = lax.div(hd, 2), lax.rem(hd, 2)

    def to_head(j):
        return {"head": j}

    def to_y(j):
        return {"ctx": z * ny + j}

    def to_z(j):
        return {"ctx": j * ny + y}

    def remote(src, dst, send, recv, where):
        return pltpu.make_async_remote_copy(
            src_ref=src, dst_ref=dst, send_sem=send, recv_sem=recv,
            device_id=where, device_id_type=MESH,
        )

    def bit(v, m):
        return lax.rem(lax.div(v, 1 << m), 2) == 1

    hops = sorted(range(1, nh // 2), key=lambda o: -min(o, nh // 2 - o))
    chips_round = [lax.rem(chip + o, nh // 2) for o in hops]
    heads_round = []
    for q in chips_round:
        heads_round += [2 * q + core, 2 * q + 1 - core]
    heads_round.append(2 * chip + 1 - core)
    y_round = [lax.rem(y + i, ny) for i in far_first(ny)]
    z_round = [lax.rem(z + i, nz) for i in range(1, nz)]

    lt[...] = jnp.zeros_like(lt)
    barrier = pltpu.get_barrier_semaphore()
    for j in heads_round:
        pl.semaphore_signal(barrier, inc=1, device_id=to_head(j), device_id_type=MESH)
    for j in y_round:
        pl.semaphore_signal(barrier, inc=1, device_id=to_y(j), device_id_type=MESH)
    for j in z_round:
        pl.semaphore_signal(barrier, inc=1, device_id=to_z(j), device_id_type=MESH)

    loads = [
        pltpu.make_async_copy(src, dst, ins.at[i])
        for i, (src, dst) in enumerate((
            (d_in, d), (x_in, x), (b_in, br.at[hd]), (c_in, cr.at[hd]),
            (codes_in, codes), (tab_in, tab), (skip_in, skip),
        ))
    ]
    for load in loads:
        load.start()
    b, c = br.at[hd], cr.at[hd]

    loads[0].wait()
    lower = iota((SPAN, SPAN), 0) >= iota((SPAN, SPAN), 1)
    run = dot(jnp.where(lower, 1.0, 0.0).astype(BF16), d[...])
    tot = run[SPAN - 1:SPAN, :]
    fac = jnp.exp(tot - run)

    def carry(ch, j):
        def one(p, _):
            cols = pl.ds(pl.multiple_of(p * LANES, LANES), LANES)
            at = j * groups + ch * gc + p
            src = pl.ds(pl.multiple_of(at * LANES, LANES), LANES)
            m = spread(fac, 2 * at)
            xc[ch, j, :, cols] = (m * x[:, src].astype(F32)).astype(BF16)
            return 0

        lax.fori_loop(0, gc, one, 0, unroll=4)

    def move_x(ch, j, src):
        return remote(
            xc.at[ch, j], xr.at[ch, src], xs.at[0, ch, j], xs.at[1, ch, src], to_head(j)
        )

    def move_b(j, src):
        return remote(b, br.at[src], bs.at[0, j], bs.at[1, src], to_head(j))

    def move_c(j, src):
        return remote(c, cr.at[src], cs.at[0, j], cs.at[1, src], to_head(j))

    def move_a(j, src):
        return remote(aux.at[j], auxr.at[src], axs.at[0, j], axs.at[1, src], to_head(j))

    def move_o(ch, j, src):
        return remote(
            io.at[ch, j], ir.at[ch, src], ios.at[0, ch, j], ios.at[1, ch, src], to_head(j)
        )

    def share_aux():
        pairs = HEADS // 2
        first = 2 * iota((pairs, LANES), 0) + (iota((pairs, LANES), 1) >> 6)
        tot_pairs = jnp.take_along_axis(
            jnp.broadcast_to(tot, (pairs, LANES)), first, axis=1, mode="promise_in_bounds"
        )
        code_row = codes[...].astype(F32)
        for j in range(nh):
            aux[j, 0:groups, :] = tot_pairs[j * groups:(j + 1) * groups, :]
            aux[j, groups:groups + 8, 0:SPAN] = jnp.broadcast_to(code_row, (8, SPAN))
            aux[j, groups:groups + 8, SPAN:] = jnp.zeros((8, LANES - SPAN), F32)
        auxr[hd] = aux[hd]
        for j in heads_round:
            move_a(j, hd).start()

    for load in loads[1:]:
        load.wait()
    carry(0, heads_round[0])
    pl.semaphore_wait(barrier, (nh - 1) + (ny - 1) + (nz - 1))
    for ch in chunks:
        for i, j in enumerate(heads_round):
            if i or ch:
                carry(ch, j)
            move_x(ch, j, hd).start()
            if ch == 0:
                move_b(j, hd).start()
        if ch == 0:
            share_aux()
    for j in heads_round:
        move_c(j, hd).start()
    for ch in chunks:
        carry(ch, hd)
        xr[ch, hd] = xc[ch, hd]

    for j in heads_round:
        move_a(j, j).wait_recv()
    mine = auxr[0, 0:groups, :]
    for g in range(nh):
        pg[g] = jnp.exp(mine) if g else jnp.ones((groups, LANES), F32)
        if g:
            mine = mine + auxr[g, 0:groups, :]
    tau[y] = mine

    def move_tau(j, src):
        return remote(tau.at[y], tau.at[src], taus.at[0, j], taus.at[1, src], to_y(j))

    for j in y_round:
        move_tau(j, y).start()

    cols0 = iota((LEVELS * HEADS, LANES), 0)
    lane0 = iota((LEVELS * HEADS, LANES), 1)
    tab0 = dot(tab[...], jnp.where(cols0 == lane0 * LEVELS, 1.0, 0.0).astype(BF16)).astype(BF16)
    code_row = codes[...].astype(F32)
    code_t = jnp.where(
        jnp.broadcast_to(code_row, (CODES, SPAN)) == iota((CODES, SPAN), 0).astype(F32), 1.0, 0.0
    ).astype(BF16)
    w0 = dot_t(code_t, tab0)
    rows[0] = w0 * jnp.exp(run - tot)
    rows[1] = jnp.exp(run)

    per = LANES // hl
    for t in range(-(-nlev // per)):
        lev = 1 + t * per + lane0 // hl
        want = (hd * hl + lax.rem(lane0, hl)) * LEVELS + lev
        picked = dot(tab[...], jnp.where(cols0 == want, 1.0, 0.0).astype(BF16))
        for l in range(t * per, min(nlev, (t + 1) * per)):
            for p in range(groups):
                te[l, :, p * LANES:(p + 1) * LANES] = spread(
                    picked, (l - t * per) * hl + 2 * p
                ).astype(BF16)
    eye = jnp.where(iota((CODES, CODES), 0) == iota((CODES, CODES), 1), 1.0, 0.0).astype(BF16)
    for g in range(nh):
        row = auxr[g, groups:groups + 1, 0:SPAN]
        hot = jnp.where(
            jnp.broadcast_to(row, (CODES, SPAN)) == iota((CODES, SPAN), 0).astype(F32), 1.0, 0.0
        ).astype(BF16)
        oh[g * SPAN:(g + 1) * SPAN, :] = dot_t(hot, eye).astype(BF16)

    scores = lax.dot_general(
        c[...], b[...], (((1,), (1,)), ((), ())), preferred_element_type=F32
    )
    near = jnp.where(lower, scores, 0.0).astype(BF16)
    gain = jnp.broadcast_to(skip[...], (SPAN, LANES))

    def level0(j, _):
        for ch in chunks:
            v = dot(near, xc[ch, j])
            for p in range(gc):
                at = j * groups + ch * gc + p
                cols = pl.ds(pl.multiple_of(at * LANES, LANES), LANES)
                o0[:, cols] = (
                    spread(rows[0], 2 * at) * v[:, p * LANES:(p + 1) * LANES]
                    + spread(gain, 2 * at) * x[:, cols].astype(F32)
                )
        return 0

    lax.fori_loop(0, nh, level0, 0)

    for j in y_round:
        move_tau(j, j).wait_recv()
    line = tau[0]
    for j in range(1, ny):
        line = line + tau[j]
    lt[z] = line

    def send_lt(i):
        return remote(lt.at[z], lt.at[z], lts.at[0, z + i], lts.at[1, z], to_z(z + i))

    def recv_lt(i):
        return remote(lt.at[z], lt.at[z - i], lts.at[0, z], lts.at[1, z - i], to_z(z - i))

    for i in range(1, nz):
        @pl.when(z + i < nz)
        def _():
            send_lt(i).start()

    def weigh(l, cols, g0, g1):
        w = dot(oh[g0 * SPAN:g1 * SPAN, :], te[l, :, cols]).astype(BF16)
        for t in range(g0 // 2, g1 // 2):
            we[l, t, :, cols] = w[(2 * t - g0) * SPAN:(2 * t + 2 - g0) * SPAN]

    for l in range(nlev):
        for i in range(0, groups * LANES, TILE):
            if l < hbits and l > 0:
                for g in range(2 << l >> 1, nh, 2 << l):
                    weigh(l, slice(i, i + TILE), g, g + (1 << l))
            else:
                weigh(l, slice(i, i + TILE), 0, nh)

    offs = [0]
    for m in range(hbits):
        offs.append(offs[-1] + (nh >> (m + 1)))

    def fold(ch):
        def one(p, _):
            cols = pl.ds(pl.multiple_of(p * LANES, LANES), LANES)
            cur = [sg[g, :, cols] for g in range(nh)]
            dec = [auxr[g, pl.ds(ch * gc + p, 1), :] for g in range(nh)]
            for m in range(hbits):
                new, new_dec = [], []
                for i in range(len(cur) // 2):
                    lbs[ch, offs[m] + i, :, cols] = cur[2 * i].astype(BF16)
                    new.append(cur[2 * i] * jnp.exp(dec[2 * i + 1]) + cur[2 * i + 1])
                    new_dec.append(dec[2 * i] + dec[2 * i + 1])
                cur, dec = new, new_dec
            for r in range(SPLIT):
                sb[ch, p * SPLIT + r] = cur[0][r * rp:(r + 1) * rp].astype(BF16)
            return 0

        lax.fori_loop(0, gc, one, 0)

    def move_r1(ch, j, src):
        return remote(
            sb.at[ch, pl.ds(j * up, up)], r1.at[ch, src],
            r1s.at[0, ch, j], r1s.at[1, ch, src], to_y(j),
        )

    def move_l0(ch, j):
        return remote(sb.at[ch], yb.at[ch, 0], l0s.at[0, ch], l0s.at[1, ch], to_y(j))

    for ch in chunks:
        sg[hd] = dot_t(br[hd], xr[ch, hd])
        for j in reversed(heads_round):
            if ch == 0:
                move_b(j, j).wait_recv()
            move_x(ch, j, j).wait_recv()
            sg[j] = dot_t(br[j], xr[ch, j])
        fold(ch)
        for j in y_round:
            move_r1(ch, j, y).start()

        for q in range(up):
            r1[ch, y, q] = sb[ch, y * up + q]

    for i in range(1, nz):
        @pl.when(z - i >= 0)
        def _():
            recv_lt(i).wait_recv()

    yoffs = [0]
    for m in range(1, ybits):
        yoffs.append(yoffs[-1] + (ny >> (m + 1)))

    def row_of(ch, q):
        return pl.ds(ch * gc + lax.div(y * up + q, SPLIT), 1)

    def send_r2(ch, i):
        return remote(
            tz.at[ch], r2.at[ch, z], r2s.at[0, ch, z + i], r2s.at[1, ch, z], to_z(z + i)
        )

    def recv_r2(ch, i):
        return remote(
            tz.at[ch], r2.at[ch, z - i], r2s.at[0, ch, z], r2s.at[1, ch, z - i], to_z(z - i)
        )

    def move_yb(ch, m, j, src):
        return remote(
            pb.at[ch, yoffs[m - 1] + lax.div(j, 2 << m)], yb.at[ch, m, pl.ds(src * up, up)],
            ys.at[0, ch, m, j], ys.at[1, ch, m, src], to_y(j),
        )

    def line_sums(ch):
        for j in y_round:
            move_r1(ch, j, j).wait_recv()
        for q in range(up):
            cur = [r1[ch, j, q].astype(F32) for j in range(ny)]
            dec = [tau[j, row_of(ch, q), :] for j in range(ny)]
            for m in range(ybits):
                new, new_dec = [], []
                for i in range(len(cur) // 2):
                    if m:
                        pb[ch, yoffs[m - 1] + i, q] = cur[2 * i].astype(BF16)
                    new.append(cur[2 * i] * jnp.exp(dec[2 * i + 1]) + cur[2 * i + 1])
                    new_dec.append(dec[2 * i] + dec[2 * i + 1])
                cur, dec = new, new_dec
            r2[ch, z, q] = cur[0].astype(BF16)
            tz[ch, q] = cur[0].astype(BF16)
        for i in far_first(nz):
            @pl.when(z + i < nz)
            def _():
                send_r2(ch, i).start()

    def share_y(ch, m):
        if m == 0:
            @pl.when(lax.rem(y, 2) == 0)
            def _():
                move_l0(ch, y + 1).start()
        elif m < ybits:
            for j in y_round:
                @pl.when(bit(j, m))
                def _():
                    move_yb(ch, m, j, y).start()

            @pl.when(bit(y, m))
            def _():
                for q in range(up):
                    yb[ch, m, y * up + q] = pb[ch, yoffs[m - 1] + lax.div(y, 2 << m), q]

    line_sums(0)
    for m in range(3):
        share_y(0, m)
    line_sums(1)

    for j in heads_round:
        move_c(j, j).wait_recv()

    def cpair(t):
        return cr[pl.ds(2 * t, 2)].reshape(2 * SPAN, STATE)

    def scaled(v, row0, row1):
        return jnp.concatenate([v[:SPAN] * row0, v[SPAN:] * row1], axis=0)

    def gap_rows(lo, g):
        gap = jnp.zeros((groups, LANES), F32)
        for before in range(lo, g):
            gap = gap + auxr[before, 0:groups, :]
        return jnp.exp(gap)

    def wide_rows(tile, ch, cols):
        at = [ch * gc + i // LANES for i in range(cols.start, cols.stop, LANES)]
        return jnp.concatenate([tile[i:i + 1, :] for i in at], axis=1)

    def inner(ch):
        for t in range(nh // 2):
            cp = cpair(t)
            for cols in tiles:
                full = slice(ch * wc + cols.start, ch * wc + cols.stop)
                v = dot(cp[SPAN:], lbs[ch, t, :, cols]) * we[0, t, SPAN:, full].astype(F32)
                acc = None
                for m in range(1, hbits):
                    if not 2 * t >> m & 1:
                        continue
                    lo = 2 * t >> m << m
                    term = we[m, t, :, full].astype(F32) * dot(
                        cp, lbs[ch, offs[m] + (2 * t >> (m + 1)), :, cols]
                    )
                    term = scaled(
                        term,
                        wide_rows(gap_rows(lo, 2 * t), ch, cols),
                        wide_rows(gap_rows(lo, 2 * t + 1), ch, cols),
                    )
                    acc = term if acc is None else acc + term
                if acc is None:
                    li[t, :SPAN, full] = jnp.zeros((SPAN, TILE), F32)
                    li[t, SPAN:, full] = v
                else:
                    li[t, :SPAN, full] = acc[:SPAN]
                    li[t, SPAN:, full] = acc[SPAN:] + v

    for ch in chunks:
        inner(ch)

    right, left = lax.rem(y + 1, ny), lax.rem(y + ny - 1, ny)
    steps = (ny - 1 - ny // 2, ny // 2)

    def hop(ch, m, way, s):
        own = lax.rem(y + ny - s, ny) if way == 0 else lax.rem(y + s, ny)
        part = zb.at[ch, m, pl.ds(own * up, up)]
        return remote(
            part, part, ags.at[0, ch, m, way, s], ags.at[1, ch, m, way, s],
            to_y(right if way == 0 else left),
        )

    def landed(ch, m, way, s):
        own = lax.rem(y + ny - s - 1, ny) if way == 0 else lax.rem(y + s + 1, ny)
        part = zb.at[ch, m, pl.ds(own * up, up)]
        return remote(
            part, part, ags.at[0, ch, m, way, s], ags.at[1, ch, m, way, s],
            to_y(left if way == 0 else right),
        )

    def pass_on(ch, s):
        for m in range(zbits):
            @pl.when(bit(z, m))
            def _():
                for way in range(2):
                    if s < steps[way]:
                        if s:
                            landed(ch, m, way, s - 1).wait_recv()
                        hop(ch, m, way, s).start()

    def before_y(lo):
        gap = jnp.zeros((groups, LANES), F32)
        for j in range(ny):
            gap = gap + jnp.where(jnp.logical_and(j >= lo, j < y), tau[j], 0.0)
        return gap

    def before_z(lo):
        gap = jnp.zeros((groups, LANES), F32)
        for j in range(nz):
            gap = gap + jnp.where(jnp.logical_and(j >= lo, j < z), lt[j], 0.0)
        return gap

    def put(ch, slot, part, gap):
        scale = jnp.exp(gap)
        for p in range(gc):
            for r in range(SPLIT):
                bks[ch, slot, r * rp:(r + 1) * rp, p * LANES:(p + 1) * LANES] = (
                    part[p * SPLIT + r].astype(F32) * scale[ch * gc + p:ch * gc + p + 1, :]
                ).astype(BF16)

    def put_y(ch):
        for m in range(ybits):
            @pl.when(bit(y, m))
            def _():
                if m == 0:
                    move_l0(ch, y - 1).wait_recv()
                else:
                    for j in y_round:
                        move_yb(ch, m, j, j).wait_recv()
                put(ch, m, yb.at[ch, m], before_y(lax.div(y, 1 << m) * (1 << m)))

            @pl.when(jnp.logical_not(bit(y, m)))
            def _():
                bks[ch, m] = jnp.zeros((STATE, wc), BF16)

    def put_z(ch):
        for m in range(zbits):
            @pl.when(bit(z, m))
            def _():
                for way in range(2):
                    if steps[way]:
                        landed(ch, m, way, steps[way] - 1).wait_recv()
                put(
                    ch, ybits + m, zb.at[ch, m],
                    before_y(0) + before_z(lax.div(z, 1 << m) * (1 << m)),
                )

            @pl.when(jnp.logical_not(bit(z, m)))
            def _():
                bks[ch, ybits + m] = jnp.zeros((STATE, wc), BF16)

    def cross(ch, t, cols, levels):
        full = slice(ch * wc + cols.start, ch * wc + cols.stop)
        cp = cpair(t)
        acc = None
        for m in levels:
            term = we[hbits + m, t, :, full].astype(F32) * dot(cp, bks[ch, m, :, cols])
            acc = term if acc is None else acc + term
        acc = scaled(
            acc, wide_rows(pg[2 * t], ch, cols), wide_rows(pg[2 * t + 1], ch, cols)
        )
        return acc + li[t, :, full]

    def cross_y(ch):
        def one(t, _):
            for cols in tiles:
                full = slice(ch * wc + cols.start, ch * wc + cols.stop)
                li[t, :, full] = cross(ch, t, cols, range(ybits))
            return 0

        lax.fori_loop(0, nh // 2, one, 0)

    def cross_z(ch, t):
        for cols in tiles:
            v = cross(ch, t, cols, range(ybits, ybits + zbits)).astype(BF16)
            io[ch, 2 * t, :, cols] = v[:SPAN]
            io[ch, 2 * t + 1, :, cols] = v[SPAN:]

    def return_rows():
        def one(p, _):
            cols = pl.ds(pl.multiple_of(p * LANES, LANES), LANES)
            er[:, cols] = spread(rows[1], 2 * p)
            return 0

        lax.fori_loop(0, HEADS // 2, one, 0, unroll=4)

    def z_sums(ch):
        for i in range(1, nz):
            @pl.when(z - i >= 0)
            def _():
                recv_r2(ch, i).wait_recv()
        for m in range(zbits):
            @pl.when(bit(z, m))
            def _():
                base = lax.div(z, 1 << m) * (1 << m)
                for q in range(up):
                    acc = r2[ch, base - 1, q].astype(F32)
                    gap = lt[base - 1, row_of(ch, q), :]
                    for i in range(2, (1 << m) + 1):
                        acc = acc + r2[ch, base - i, q].astype(F32) * jnp.exp(gap)
                        gap = gap + lt[base - i, row_of(ch, q), :]
                    zb[ch, m, y * up + q] = acc.astype(BF16)
        pass_on(ch, 0)

    def give_back(ch, i):
        if i < len(chips_round):
            cross_z(ch, chips_round[i])
            for j in heads_round[2 * i:2 * i + 2]:
                move_o(ch, j, hd).start()
        elif i == len(chips_round):
            cross_z(ch, chip)
            move_o(ch, heads_round[-1], hd).start()
            ir[ch, hd] = io[ch, hd]

    z_sums(0)
    share_y(1, 0)
    return_rows()
    pass_on(0, 1)
    share_y(1, 1)
    put_y(0)
    cross_y(0)
    pass_on(0, 2)
    share_y(1, 2)
    z_sums(1)
    pass_on(0, 3)
    pass_on(1, 1)
    put_y(1)
    cross_y(1)
    pass_on(1, 2)
    put_z(0)
    give_back(0, 0)
    give_back(0, 1)
    pass_on(1, 3)
    give_back(0, 2)
    give_back(0, 3)
    put_z(1)
    for i in range(4):
        give_back(1, i)

    def finish(ch, j):
        def one(p, _):
            at = j * groups + ch * gc + p
            cols = pl.ds(pl.multiple_of(at * LANES, LANES), LANES)
            part = pl.ds(pl.multiple_of(p * LANES, LANES), LANES)
            out[:, cols] = (
                o0[:, cols] + er[:, cols] * ir[ch, j, :, part].astype(F32)
            ).astype(BF16)
            return 0

        lax.fori_loop(0, gc, one, 0, unroll=4)

    for ch in chunks:
        finish(ch, hd)
        for j in heads_round[::-1]:
            move_o(ch, j, j).wait_recv()
            finish(ch, j)

    for j in heads_round:
        move_a(j, hd).wait_send()
        move_b(j, hd).wait_send()
        move_c(j, hd).wait_send()
        for ch in chunks:
            move_x(ch, j, hd).wait_send()
            move_o(ch, j, hd).wait_send()
    for j in y_round:
        move_tau(j, y).wait_send()
        for ch in chunks:
            move_r1(ch, j, y).wait_send()
        for m in range(1, ybits):
            @pl.when(bit(j, m))
            def _():
                for ch in chunks:
                    move_yb(ch, m, j, y).wait_send()

    @pl.when(lax.rem(y, 2) == 0)
    def _():
        for ch in chunks:
            move_l0(ch, y + 1).wait_send()

    for i in range(1, nz):
        @pl.when(z + i < nz)
        def _():
            send_lt(i).wait_send()
            for ch in chunks:
                send_r2(ch, i).wait_send()
    for s in range(max(steps)):
        for m in range(zbits):
            @pl.when(bit(z, m))
            def _():
                for ch in chunks:
                    for way in range(2):
                        if s < steps[way]:
                            hop(ch, m, way, s).wait_send()


def on_device(nh, ny, nz, token_inputs, state_in, state_out, log_decay, token_codes, table, gain):
    hl = HEADS // nh
    groups = hl // 2
    gc = groups // CHUNKS
    units = gc * SPLIT
    up = units // ny
    rp = STATE // SPLIT
    wide = hl * HEAD_DIM
    wc = wide // CHUNKS
    hbits, ybits, zbits = bits_of(nh), bits_of(ny), bits_of(nz)
    nlev = hbits + ybits + zbits
    vm = pltpu.VMEM
    sem = pltpu.SemaphoreType.DMA
    pieces = max(sum(ny >> (m + 1) for m in range(1, ybits)), 1)
    nc = CHUNKS
    zb = max(zbits, 1)
    return pl.pallas_call(
        functools.partial(kernel, nh, ny, nz),
        out_shape=jax.ShapeDtypeStruct((SPAN, HEADS * HEAD_DIM), BF16),
        in_specs=[pl.BlockSpec(memory_space=pltpu.HBM)] * 7,
        out_specs=pl.BlockSpec(memory_space=pltpu.VMEM),
        scratch_shapes=[
            vm((SPAN, HEADS * HEAD_DIM), BF16),
            vm((SPAN, HEADS), BF16),
            vm((1, SPAN), jnp.int32),
            vm((CODES, LEVELS * HEADS), BF16),
            vm((1, HEADS), F32),
            vm((nc, nh, SPAN, wc), BF16),
            vm((nc, nh, SPAN, wc), BF16),
            vm((nh, SPAN, STATE), BF16),
            vm((nh, SPAN, STATE), BF16),
            vm((nh, groups + 8, LANES), F32),
            vm((nh, groups + 8, LANES), F32),
            vm((SPAN, HEADS * HEAD_DIM), F32),
            vm((SPAN, HEADS * HEAD_DIM), F32),
            vm((2, SPAN, LANES), F32),
            vm((nlev, CODES, wide), BF16),
            vm((nh * SPAN, CODES), BF16),
            vm((nlev, nh // 2, 2 * SPAN, wide), BF16),
            vm((nh, STATE, wc), F32),
            vm((nc, nh - 1, STATE, wc), BF16),
            vm((nh // 2, 2 * SPAN, wide), F32),
            vm((nc, units, rp, LANES), BF16),
            vm((nc, ny, up, rp, LANES), BF16),
            vm((nc, pieces, up, rp, LANES), BF16),
            vm((nc, up, rp, LANES), BF16),
            vm((nc, nz, up, rp, LANES), BF16),
            vm((nc, ybits, units, rp, LANES), BF16),
            vm((nc, zb, units, rp, LANES), BF16),
            vm((nc, ybits + zbits, STATE, wc), BF16),
            vm((ny, groups, LANES), F32),
            vm((nz, groups, LANES), F32),
            vm((nh, groups, LANES), F32),
            vm((nc, nh, SPAN, wc), BF16),
            vm((nc, nh, SPAN, wc), BF16),
            sem((7,)),
            sem((2, nc, nh)),
            sem((2, nh)),
            sem((2, nh)),
            sem((2, nh)),
            sem((2, ny)),
            sem((2, nz)),
            sem((2, nc, ny)),
            sem((2, nc)),
            sem((2, nc, max(ybits, 1), ny)),
            sem((2, nc, nz)),
            sem((2, nc, zb, 2, max(ny // 2, 1))),
            sem((2, nc, nh)),
        ],
        compiler_params=pltpu.CompilerParams(
            collective_id=0, has_side_effects=True, vmem_limit_bytes=VMEM_LIMIT
        ),
    )(*(
        pltpu.with_memory_space_constraint(v, pltpu.HBM)
        for v in (
            token_inputs, state_in, state_out, log_decay,
            token_codes.reshape(1, SPAN), table, gain.reshape(1, HEADS),
        )
    ))


def solution(mesh, ny=NY):
    nh = mesh.shape["head"]
    nz = mesh.shape["ctx"] // ny
    return jax.shard_map(
        functools.partial(on_device, nh, ny, nz),
        mesh=mesh,
        in_specs=(
            P(("ctx", "head"), None),
            P(("ctx", "head"), None),
            P(("ctx", "head"), None),
            P(("ctx", "head"), None),
            P(("ctx", "head")),
            P(),
            P(),
        ),
        out_specs=P(("ctx", "head"), None),
        check_vma=False,
    )
```

```python
import functools

import jax
import jax.numpy as jnp
from jax import lax
from jax.experimental import pallas as pl
from jax.experimental.pallas import tpu as pltpu
from jax.sharding import PartitionSpec as P

HEADS = 128
HEAD_DIM = 64
STATE = 128
SPAN = 64
LEVELS = 11
CODES = 64
NY = 8
LANES = 128
CHUNKS = 2
SPLIT = 2
TILE = 256
VMEM_LIMIT = 44 << 20
MESH = pl.DeviceIdType.MESH
F32 = jnp.float32
BF16 = jnp.bfloat16


def bits_of(n):
    return n.bit_length() - 1


def far_first(n):
    return sorted(range(1, n), key=lambda i: -min(i, n - i))


def dot(a, b):
    return jnp.dot(a, b, preferred_element_type=F32)


def dot_t(a, b):
    return lax.dot_general(a, b, (((0,), (0,)), ((), ())), preferred_element_type=F32)


def iota(shape, dim):
    return lax.broadcasted_iota(jnp.int32, shape, dim)


def spread(v, first):
    idx = first + (iota(v.shape, 1) >> 6)
    return jnp.take_along_axis(v, idx, axis=1, mode="promise_in_bounds")


def kernel(
    nh, ny, nz,
    x_in, b_in, c_in, d_in, codes_in, tab_in, skip_in, out,
    x, d, codes, tab, skip,
    xc, xr, br, cr, aux, auxr, o0, er, rows, te, oh, we, sg, lbs, li,
    sb, r1, pb, tz, r2, yb, zb, bks, tau, lt, pg, io, ir,
    ins, xs, bs, cs, axs, taus, lts, r1s, l0s, ys, r2s, ags, ios,
):
    hl = HEADS // nh
    groups = hl // 2
    gc = groups // CHUNKS
    units = gc * SPLIT
    up = units // ny
    rp = STATE // SPLIT
    wc = gc * LANES
    tiles = [slice(i, i + TILE) for i in range(0, wc, TILE)]
    hbits, ybits, zbits = bits_of(nh), bits_of(ny), bits_of(nz)
    nlev = hbits + ybits + zbits
    chunks = range(CHUNKS)
    hd = lax.axis_index("head")
    k = lax.axis_index("ctx")
    y = lax.rem(k, ny)
    z = lax.div(k, ny)
    chip, core = lax.div(hd, 2), lax.rem(hd, 2)

    def to_head(j):
        return {"head": j}

    def to_y(j):
        return {"ctx": z * ny + j}

    def to_z(j):
        return {"ctx": j * ny + y}

    def remote(src, dst, send, recv, where):
        return pltpu.make_async_remote_copy(
            src_ref=src, dst_ref=dst, send_sem=send, recv_sem=recv,
            device_id=where, device_id_type=MESH,
        )

    def bit(v, m):
        return lax.rem(lax.div(v, 1 << m), 2) == 1

    hops = sorted(range(1, nh // 2), key=lambda o: -min(o, nh // 2 - o))
    chips_round = [lax.rem(chip + o, nh // 2) for o in hops]
    heads_round = []
    for q in chips_round:
        heads_round += [2 * q + core, 2 * q + 1 - core]
    heads_round.append(2 * chip + 1 - core)
    y_round = [lax.rem(y + i, ny) for i in far_first(ny)]
    z_round = [lax.rem(z + i, nz) for i in range(1, nz)]

    lt[...] = jnp.zeros_like(lt)
    barrier = pltpu.get_barrier_semaphore()
    for j in heads_round:
        pl.semaphore_signal(barrier, inc=1, device_id=to_head(j), device_id_type=MESH)
    for j in y_round:
        pl.semaphore_signal(barrier, inc=1, device_id=to_y(j), device_id_type=MESH)
    for j in z_round:
        pl.semaphore_signal(barrier, inc=1, device_id=to_z(j), device_id_type=MESH)

    loads = [
        pltpu.make_async_copy(src, dst, ins.at[i])
        for i, (src, dst) in enumerate((
            (d_in, d), (x_in, x), (b_in, br.at[hd]), (c_in, cr.at[hd]),
            (codes_in, codes), (tab_in, tab), (skip_in, skip),
        ))
    ]
    for load in loads:
        load.start()
    b, c = br.at[hd], cr.at[hd]

    loads[0].wait()
    lower = iota((SPAN, SPAN), 0) >= iota((SPAN, SPAN), 1)
    run = dot(jnp.where(lower, 1.0, 0.0).astype(BF16), d[...])
    tot = run[SPAN - 1:SPAN, :]
    fac = jnp.exp(tot - run)

    def carry(ch, j):
        def one(p, _):
            cols = pl.ds(pl.multiple_of(p * LANES, LANES), LANES)
            at = j * groups + ch * gc + p
            src = pl.ds(pl.multiple_of(at * LANES, LANES), LANES)
            m = spread(fac, 2 * at)
            xc[ch, j, :, cols] = (m * x[:, src].astype(F32)).astype(BF16)
            return 0

        lax.fori_loop(0, gc, one, 0, unroll=4)

    def move_x(ch, j, src):
        return remote(
            xc.at[ch, j], xr.at[ch, src], xs.at[0, ch, j], xs.at[1, ch, src], to_head(j)
        )

    def move_b(j, src):
        return remote(b, br.at[src], bs.at[0, j], bs.at[1, src], to_head(j))

    def move_c(j, src):
        return remote(c, cr.at[src], cs.at[0, j], cs.at[1, src], to_head(j))

    def move_a(j, src):
        return remote(aux.at[j], auxr.at[src], axs.at[0, j], axs.at[1, src], to_head(j))

    def move_o(ch, j, src):
        return remote(
            io.at[ch, j], ir.at[ch, src], ios.at[0, ch, j], ios.at[1, ch, src], to_head(j)
        )

    def share_aux():
        pairs = HEADS // 2
        first = 2 * iota((pairs, LANES), 0) + (iota((pairs, LANES), 1) >> 6)
        tot_pairs = jnp.take_along_axis(
            jnp.broadcast_to(tot, (pairs, LANES)), first, axis=1, mode="promise_in_bounds"
        )
        code_row = codes[...].astype(F32)
        for j in range(nh):
            aux[j, 0:groups, :] = tot_pairs[j * groups:(j + 1) * groups, :]
            aux[j, groups:groups + 8, 0:SPAN] = jnp.broadcast_to(code_row, (8, SPAN))
            aux[j, groups:groups + 8, SPAN:] = jnp.zeros((8, LANES - SPAN), F32)
        auxr[hd] = aux[hd]
        for j in heads_round:
            move_a(j, hd).start()

    for load in loads[1:]:
        load.wait()
    carry(0, heads_round[0])
    pl.semaphore_wait(barrier, (nh - 1) + (ny - 1) + (nz - 1))
    for ch in chunks:
        for i, j in enumerate(heads_round):
            if i or ch:
                carry(ch, j)
            move_x(ch, j, hd).start()
            if ch == 0:
                move_b(j, hd).start()
        if ch == 0:
            share_aux()
    for j in heads_round:
        move_c(j, hd).start()
    for ch in chunks:
        carry(ch, hd)
        xr[ch, hd] = xc[ch, hd]

    for j in heads_round:
        move_a(j, j).wait_recv()
    mine = auxr[0, 0:groups, :]
    for g in range(nh):
        pg[g] = jnp.exp(mine) if g else jnp.ones((groups, LANES), F32)
        if g:
            mine = mine + auxr[g, 0:groups, :]
    tau[y] = mine

    def move_tau(j, src):
        return remote(tau.at[y], tau.at[src], taus.at[0, j], taus.at[1, src], to_y(j))

    for j in y_round:
        move_tau(j, y).start()

    cols0 = iota((LEVELS * HEADS, LANES), 0)
    lane0 = iota((LEVELS * HEADS, LANES), 1)
    tab0 = dot(tab[...], jnp.where(cols0 == lane0 * LEVELS, 1.0, 0.0).astype(BF16)).astype(BF16)
    code_row = codes[...].astype(F32)
    code_t = jnp.where(
        jnp.broadcast_to(code_row, (CODES, SPAN)) == iota((CODES, SPAN), 0).astype(F32), 1.0, 0.0
    ).astype(BF16)
    w0 = dot_t(code_t, tab0)
    rows[0] = w0 * jnp.exp(run - tot)
    rows[1] = jnp.exp(run)

    per = LANES // hl
    for t in range(-(-nlev // per)):
        lev = 1 + t * per + lane0 // hl
        want = (hd * hl + lax.rem(lane0, hl)) * LEVELS + lev
        picked = dot(tab[...], jnp.where(cols0 == want, 1.0, 0.0).astype(BF16))
        for l in range(t * per, min(nlev, (t + 1) * per)):
            for p in range(groups):
                te[l, :, p * LANES:(p + 1) * LANES] = spread(
                    picked, (l - t * per) * hl + 2 * p
                ).astype(BF16)
    eye = jnp.where(iota((CODES, CODES), 0) == iota((CODES, CODES), 1), 1.0, 0.0).astype(BF16)
    for g in range(nh):
        row = auxr[g, groups:groups + 1, 0:SPAN]
        hot = jnp.where(
            jnp.broadcast_to(row, (CODES, SPAN)) == iota((CODES, SPAN), 0).astype(F32), 1.0, 0.0
        ).astype(BF16)
        oh[g * SPAN:(g + 1) * SPAN, :] = dot_t(hot, eye).astype(BF16)

    scores = lax.dot_general(
        c[...], b[...], (((1,), (1,)), ((), ())), preferred_element_type=F32
    )
    near = jnp.where(lower, scores, 0.0).astype(BF16)
    gain = jnp.broadcast_to(skip[...], (SPAN, LANES))

    def level0(j, _):
        for ch in chunks:
            v = dot(near, xc[ch, j])
            for p in range(gc):
                at = j * groups + ch * gc + p
                cols = pl.ds(pl.multiple_of(at * LANES, LANES), LANES)
                o0[:, cols] = (
                    spread(rows[0], 2 * at) * v[:, p * LANES:(p + 1) * LANES]
                    + spread(gain, 2 * at) * x[:, cols].astype(F32)
                )
        return 0

    lax.fori_loop(0, nh, level0, 0)

    for j in y_round:
        move_tau(j, j).wait_recv()
    line = tau[0]
    for j in range(1, ny):
        line = line + tau[j]
    lt[z] = line

    def send_lt(i):
        return remote(lt.at[z], lt.at[z], lts.at[0, z + i], lts.at[1, z], to_z(z + i))

    def recv_lt(i):
        return remote(lt.at[z], lt.at[z - i], lts.at[0, z], lts.at[1, z - i], to_z(z - i))

    for i in range(1, nz):
        @pl.when(z + i < nz)
        def _():
            send_lt(i).start()

    def weigh(l, cols, g0, g1):
        w = dot(oh[g0 * SPAN:g1 * SPAN, :], te[l, :, cols]).astype(BF16)
        for t in range(g0 // 2, g1 // 2):
            we[l, t, :, cols] = w[(2 * t - g0) * SPAN:(2 * t + 2 - g0) * SPAN]

    for l in range(nlev):
        for i in range(0, groups * LANES, TILE):
            if l < hbits and l > 0:
                for g in range(2 << l >> 1, nh, 2 << l):
                    weigh(l, slice(i, i + TILE), g, g + (1 << l))
            else:
                weigh(l, slice(i, i + TILE), 0, nh)

    offs = [0]
    for m in range(hbits):
        offs.append(offs[-1] + (nh >> (m + 1)))

    def fold(ch):
        def one(p, _):
            cols = pl.ds(pl.multiple_of(p * LANES, LANES), LANES)
            cur = [sg[g, :, cols] for g in range(nh)]
            dec = [auxr[g, pl.ds(ch * gc + p, 1), :] for g in range(nh)]
            for m in range(hbits):
                new, new_dec = [], []
                for i in range(len(cur) // 2):
                    lbs[ch, offs[m] + i, :, cols] = cur[2 * i].astype(BF16)
                    new.append(cur[2 * i] * jnp.exp(dec[2 * i + 1]) + cur[2 * i + 1])
                    new_dec.append(dec[2 * i] + dec[2 * i + 1])
                cur, dec = new, new_dec
            for r in range(SPLIT):
                sb[ch, p * SPLIT + r] = cur[0][r * rp:(r + 1) * rp].astype(BF16)
            return 0

        lax.fori_loop(0, gc, one, 0)

    def move_r1(ch, j, src):
        return remote(
            sb.at[ch, pl.ds(j * up, up)], r1.at[ch, src],
            r1s.at[0, ch, j], r1s.at[1, ch, src], to_y(j),
        )

    def move_l0(ch, j):
        return remote(sb.at[ch], yb.at[ch, 0], l0s.at[0, ch], l0s.at[1, ch], to_y(j))

    for ch in chunks:
        sg[hd] = dot_t(br[hd], xr[ch, hd])
        for j in reversed(heads_round):
            if ch == 0:
                move_b(j, j).wait_recv()
            move_x(ch, j, j).wait_recv()
            sg[j] = dot_t(br[j], xr[ch, j])
        fold(ch)
        for j in y_round:
            move_r1(ch, j, y).start()

        for q in range(up):
            r1[ch, y, q] = sb[ch, y * up + q]

    for i in range(1, nz):
        @pl.when(z - i >= 0)
        def _():
            recv_lt(i).wait_recv()

    yoffs = [0]
    for m in range(1, ybits):
        yoffs.append(yoffs[-1] + (ny >> (m + 1)))

    def row_of(ch, q):
        return pl.ds(ch * gc + lax.div(y * up + q, SPLIT), 1)

    def send_r2(ch, i):
        return remote(
            tz.at[ch], r2.at[ch, z], r2s.at[0, ch, z + i], r2s.at[1, ch, z], to_z(z + i)
        )

    def recv_r2(ch, i):
        return remote(
            tz.at[ch], r2.at[ch, z - i], r2s.at[0, ch, z], r2s.at[1, ch, z - i], to_z(z - i)
        )

    def move_yb(ch, m, j, src):
        return remote(
            pb.at[ch, yoffs[m - 1] + lax.div(j, 2 << m)], yb.at[ch, m, pl.ds(src * up, up)],
            ys.at[0, ch, m, j], ys.at[1, ch, m, src], to_y(j),
        )

    def line_sums(ch):
        for j in y_round:
            move_r1(ch, j, j).wait_recv()
        for q in range(up):
            cur = [r1[ch, j, q].astype(F32) for j in range(ny)]
            dec = [tau[j, row_of(ch, q), :] for j in range(ny)]
            for m in range(ybits):
                new, new_dec = [], []
                for i in range(len(cur) // 2):
                    if m:
                        pb[ch, yoffs[m - 1] + i, q] = cur[2 * i].astype(BF16)
                    new.append(cur[2 * i] * jnp.exp(dec[2 * i + 1]) + cur[2 * i + 1])
                    new_dec.append(dec[2 * i] + dec[2 * i + 1])
                cur, dec = new, new_dec
            r2[ch, z, q] = cur[0].astype(BF16)
            tz[ch, q] = cur[0].astype(BF16)
        for i in far_first(nz):
            @pl.when(z + i < nz)
            def _():
                send_r2(ch, i).start()

    def share_y(ch, m):
        if m == 0:
            @pl.when(lax.rem(y, 2) == 0)
            def _():
                move_l0(ch, y + 1).start()
        elif m < ybits:
            for j in y_round:
                @pl.when(bit(j, m))
                def _():
                    move_yb(ch, m, j, y).start()

            @pl.when(bit(y, m))
            def _():
                for q in range(up):
                    yb[ch, m, y * up + q] = pb[ch, yoffs[m - 1] + lax.div(y, 2 << m), q]

    line_sums(0)
    for m in range(3):
        share_y(0, m)
    line_sums(1)

    for j in heads_round:
        move_c(j, j).wait_recv()

    def cpair(t):
        return cr[pl.ds(2 * t, 2)].reshape(2 * SPAN, STATE)

    def scaled(v, row0, row1):
        return jnp.concatenate([v[:SPAN] * row0, v[SPAN:] * row1], axis=0)

    def gap_rows(lo, g):
        gap = jnp.zeros((groups, LANES), F32)
        for before in range(lo, g):
            gap = gap + auxr[before, 0:groups, :]
        return jnp.exp(gap)

    def wide_rows(tile, ch, cols):
        at = [ch * gc + i // LANES for i in range(cols.start, cols.stop, LANES)]
        return jnp.concatenate([tile[i:i + 1, :] for i in at], axis=1)

    def inner(ch):
        for t in range(nh // 2):
            cp = cpair(t)
            for cols in tiles:
                full = slice(ch * wc + cols.start, ch * wc + cols.stop)
                v = dot(cp[SPAN:], lbs[ch, t, :, cols]) * we[0, t, SPAN:, full].astype(F32)
                acc = None
                for m in range(1, hbits):
                    if not 2 * t >> m & 1:
                        continue
                    lo = 2 * t >> m << m
                    term = we[m, t, :, full].astype(F32) * dot(
                        cp, lbs[ch, offs[m] + (2 * t >> (m + 1)), :, cols]
                    )
                    term = scaled(
                        term,
                        wide_rows(gap_rows(lo, 2 * t), ch, cols),
                        wide_rows(gap_rows(lo, 2 * t + 1), ch, cols),
                    )
                    acc = term if acc is None else acc + term
                if acc is None:
                    li[t, :SPAN, full] = jnp.zeros((SPAN, TILE), F32)
                    li[t, SPAN:, full] = v
                else:
                    li[t, :SPAN, full] = acc[:SPAN]
                    li[t, SPAN:, full] = acc[SPAN:] + v

    for ch in chunks:
        inner(ch)

    right, left = lax.rem(y + 1, ny), lax.rem(y + ny - 1, ny)
    steps = (ny - 1 - ny // 2, ny // 2)

    def hop(ch, m, way, s):
        own = lax.rem(y + ny - s, ny) if way == 0 else lax.rem(y + s, ny)
        part = zb.at[ch, m, pl.ds(own * up, up)]
        return remote(
            part, part, ags.at[0, ch, m, way, s], ags.at[1, ch, m, way, s],
            to_y(right if way == 0 else left),
        )

    def landed(ch, m, way, s):
        own = lax.rem(y + ny - s - 1, ny) if way == 0 else lax.rem(y + s + 1, ny)
        part = zb.at[ch, m, pl.ds(own * up, up)]
        return remote(
            part, part, ags.at[0, ch, m, way, s], ags.at[1, ch, m, way, s],
            to_y(left if way == 0 else right),
        )

    def pass_on(ch, s):
        for m in range(zbits):
            @pl.when(bit(z, m))
            def _():
                for way in range(2):
                    if s < steps[way]:
                        if s:
                            landed(ch, m, way, s - 1).wait_recv()
                        hop(ch, m, way, s).start()

    def before_y(lo):
        gap = jnp.zeros((groups, LANES), F32)
        for j in range(ny):
            gap = gap + jnp.where(jnp.logical_and(j >= lo, j < y), tau[j], 0.0)
        return gap

    def before_z(lo):
        gap = jnp.zeros((groups, LANES), F32)
        for j in range(nz):
            gap = gap + jnp.where(jnp.logical_and(j >= lo, j < z), lt[j], 0.0)
        return gap

    def put(ch, slot, part, gap):
        scale = jnp.exp(gap)
        for p in range(gc):
            for r in range(SPLIT):
                bks[ch, slot, r * rp:(r + 1) * rp, p * LANES:(p + 1) * LANES] = (
                    part[p * SPLIT + r].astype(F32) * scale[ch * gc + p:ch * gc + p + 1, :]
                ).astype(BF16)

    def put_y(ch):
        for m in range(ybits):
            @pl.when(bit(y, m))
            def _():
                if m == 0:
                    move_l0(ch, y - 1).wait_recv()
                else:
                    for j in y_round:
                        move_yb(ch, m, j, j).wait_recv()
                put(ch, m, yb.at[ch, m], before_y(lax.div(y, 1 << m) * (1 << m)))

            @pl.when(jnp.logical_not(bit(y, m)))
            def _():
                bks[ch, m] = jnp.zeros((STATE, wc), BF16)

    def put_z(ch):
        for m in range(zbits):
            @pl.when(bit(z, m))
            def _():
                for way in range(2):
                    if steps[way]:
                        landed(ch, m, way, steps[way] - 1).wait_recv()
                put(
                    ch, ybits + m, zb.at[ch, m],
                    before_y(0) + before_z(lax.div(z, 1 << m) * (1 << m)),
                )

            @pl.when(jnp.logical_not(bit(z, m)))
            def _():
                bks[ch, ybits + m] = jnp.zeros((STATE, wc), BF16)

    def cross(ch, t, cols, levels):
        full = slice(ch * wc + cols.start, ch * wc + cols.stop)
        cp = cpair(t)
        acc = None
        for m in levels:
            term = we[hbits + m, t, :, full].astype(F32) * dot(cp, bks[ch, m, :, cols])
            acc = term if acc is None else acc + term
        acc = scaled(
            acc, wide_rows(pg[2 * t], ch, cols), wide_rows(pg[2 * t + 1], ch, cols)
        )
        return acc + li[t, :, full]

    def cross_y(ch):
        def one(t, _):
            for cols in tiles:
                full = slice(ch * wc + cols.start, ch * wc + cols.stop)
                li[t, :, full] = cross(ch, t, cols, range(ybits))
            return 0

        lax.fori_loop(0, nh // 2, one, 0)

    def cross_z(ch, t):
        for cols in tiles:
            v = cross(ch, t, cols, range(ybits, ybits + zbits)).astype(BF16)
            io[ch, 2 * t, :, cols] = v[:SPAN]
            io[ch, 2 * t + 1, :, cols] = v[SPAN:]

    def return_rows():
        def one(p, _):
            cols = pl.ds(pl.multiple_of(p * LANES, LANES), LANES)
            er[:, cols] = spread(rows[1], 2 * p)
            return 0

        lax.fori_loop(0, HEADS // 2, one, 0, unroll=4)

    def z_sums(ch):
        for i in range(1, nz):
            @pl.when(z - i >= 0)
            def _():
                recv_r2(ch, i).wait_recv()
        for m in range(zbits):
            @pl.when(bit(z, m))
            def _():
                base = lax.div(z, 1 << m) * (1 << m)
                for q in range(up):
                    acc = r2[ch, base - 1, q].astype(F32)
                    gap = lt[base - 1, row_of(ch, q), :]
                    for i in range(2, (1 << m) + 1):
                        acc = acc + r2[ch, base - i, q].astype(F32) * jnp.exp(gap)
                        gap = gap + lt[base - i, row_of(ch, q), :]
                    zb[ch, m, y * up + q] = acc.astype(BF16)
        pass_on(ch, 0)

    def give_back(ch, i):
        if i < len(chips_round):
            cross_z(ch, chips_round[i])
            for j in heads_round[2 * i:2 * i + 2]:
                move_o(ch, j, hd).start()
        elif i == len(chips_round):
            cross_z(ch, chip)
            move_o(ch, heads_round[-1], hd).start()
            ir[ch, hd] = io[ch, hd]

    z_sums(0)
    share_y(1, 0)
    return_rows()
    pass_on(0, 1)
    share_y(1, 1)
    put_y(0)
    cross_y(0)
    pass_on(0, 2)
    share_y(1, 2)
    z_sums(1)
    pass_on(0, 3)
    pass_on(1, 1)
    put_z(0)
    give_back(0, 0)
    give_back(0, 1)
    pass_on(1, 2)
    give_back(0, 2)
    give_back(0, 3)
    put_y(1)
    cross_y(1)
    pass_on(1, 3)
    put_z(1)
    for i in range(4):
        give_back(1, i)

    def finish(ch, j):
        def one(p, _):
            at = j * groups + ch * gc + p
            cols = pl.ds(pl.multiple_of(at * LANES, LANES), LANES)
            part = pl.ds(pl.multiple_of(p * LANES, LANES), LANES)
            out[:, cols] = (
                o0[:, cols] + er[:, cols] * ir[ch, j, :, part].astype(F32)
            ).astype(BF16)
            return 0

        lax.fori_loop(0, gc, one, 0, unroll=4)

    for ch in chunks:
        finish(ch, hd)
        for j in heads_round[::-1]:
            move_o(ch, j, j).wait_recv()
            finish(ch, j)

    for j in heads_round:
        move_a(j, hd).wait_send()
        move_b(j, hd).wait_send()
        move_c(j, hd).wait_send()
        for ch in chunks:
            move_x(ch, j, hd).wait_send()
            move_o(ch, j, hd).wait_send()
    for j in y_round:
        move_tau(j, y).wait_send()
        for ch in chunks:
            move_r1(ch, j, y).wait_send()
        for m in range(1, ybits):
            @pl.when(bit(j, m))
            def _():
                for ch in chunks:
                    move_yb(ch, m, j, y).wait_send()

    @pl.when(lax.rem(y, 2) == 0)
    def _():
        for ch in chunks:
            move_l0(ch, y + 1).wait_send()

    for i in range(1, nz):
        @pl.when(z + i < nz)
        def _():
            send_lt(i).wait_send()
            for ch in chunks:
                send_r2(ch, i).wait_send()
    for s in range(max(steps)):
        for m in range(zbits):
            @pl.when(bit(z, m))
            def _():
                for ch in chunks:
                    for way in range(2):
                        if s < steps[way]:
                            hop(ch, m, way, s).wait_send()


def on_device(nh, ny, nz, token_inputs, state_in, state_out, log_decay, token_codes, table, gain):
    hl = HEADS // nh
    groups = hl // 2
    gc = groups // CHUNKS
    units = gc * SPLIT
    up = units // ny
    rp = STATE // SPLIT
    wide = hl * HEAD_DIM
    wc = wide // CHUNKS
    hbits, ybits, zbits = bits_of(nh), bits_of(ny), bits_of(nz)
    nlev = hbits + ybits + zbits
    vm = pltpu.VMEM
    sem = pltpu.SemaphoreType.DMA
    pieces = max(sum(ny >> (m + 1) for m in range(1, ybits)), 1)
    nc = CHUNKS
    zb = max(zbits, 1)
    return pl.pallas_call(
        functools.partial(kernel, nh, ny, nz),
        out_shape=jax.ShapeDtypeStruct((SPAN, HEADS * HEAD_DIM), BF16),
        in_specs=[pl.BlockSpec(memory_space=pltpu.HBM)] * 7,
        out_specs=pl.BlockSpec(memory_space=pltpu.VMEM),
        scratch_shapes=[
            vm((SPAN, HEADS * HEAD_DIM), BF16),
            vm((SPAN, HEADS), BF16),
            vm((1, SPAN), jnp.int32),
            vm((CODES, LEVELS * HEADS), BF16),
            vm((1, HEADS), F32),
            vm((nc, nh, SPAN, wc), BF16),
            vm((nc, nh, SPAN, wc), BF16),
            vm((nh, SPAN, STATE), BF16),
            vm((nh, SPAN, STATE), BF16),
            vm((nh, groups + 8, LANES), F32),
            vm((nh, groups + 8, LANES), F32),
            vm((SPAN, HEADS * HEAD_DIM), F32),
            vm((SPAN, HEADS * HEAD_DIM), F32),
            vm((2, SPAN, LANES), F32),
            vm((nlev, CODES, wide), BF16),
            vm((nh * SPAN, CODES), BF16),
            vm((nlev, nh // 2, 2 * SPAN, wide), BF16),
            vm((nh, STATE, wc), F32),
            vm((nc, nh - 1, STATE, wc), BF16),
            vm((nh // 2, 2 * SPAN, wide), F32),
            vm((nc, units, rp, LANES), BF16),
            vm((nc, ny, up, rp, LANES), BF16),
            vm((nc, pieces, up, rp, LANES), BF16),
            vm((nc, up, rp, LANES), BF16),
            vm((nc, nz, up, rp, LANES), BF16),
            vm((nc, ybits, units, rp, LANES), BF16),
            vm((nc, zb, units, rp, LANES), BF16),
            vm((nc, ybits + zbits, STATE, wc), BF16),
            vm((ny, groups, LANES), F32),
            vm((nz, groups, LANES), F32),
            vm((nh, groups, LANES), F32),
            vm((nc, nh, SPAN, wc), BF16),
            vm((nc, nh, SPAN, wc), BF16),
            sem((7,)),
            sem((2, nc, nh)),
            sem((2, nh)),
            sem((2, nh)),
            sem((2, nh)),
            sem((2, ny)),
            sem((2, nz)),
            sem((2, nc, ny)),
            sem((2, nc)),
            sem((2, nc, max(ybits, 1), ny)),
            sem((2, nc, nz)),
            sem((2, nc, zb, 2, max(ny // 2, 1))),
            sem((2, nc, nh)),
        ],
        compiler_params=pltpu.CompilerParams(
            collective_id=0, has_side_effects=True, vmem_limit_bytes=VMEM_LIMIT
        ),
    )(*(
        pltpu.with_memory_space_constraint(v, pltpu.HBM)
        for v in (
            token_inputs, state_in, state_out, log_decay,
            token_codes.reshape(1, SPAN), table, gain.reshape(1, HEADS),
        )
    ))


def solution(mesh, ny=NY):
    nh = mesh.shape["head"]
    nz = mesh.shape["ctx"] // ny
    return jax.shard_map(
        functools.partial(on_device, nh, ny, nz),
        mesh=mesh,
        in_specs=(
            P(("ctx", "head"), None),
            P(("ctx", "head"), None),
            P(("ctx", "head"), None),
            P(("ctx", "head"), None),
            P(("ctx", "head")),
            P(),
            P(),
        ),
        out_specs=P(("ctx", "head"), None),
        check_vma=False,
    )
```
